32 devices in a mesh: snap: 4 (over y, x), height: 8 (over z, core).
Axes of the slice: x: 2, y: 2, z: 4, core: 2. Of those that a mesh axis runs over, the one named last changes fastest.
Arguments:
- resolved: bfloat16 [64, 3, 128, 16, 2, 128], P('snap', None, 'height'), may hold values from -6 to 6
- drain: bfloat16 [64, 3, 128, 16, 2, 128], P('snap', None, 'height'), may hold values from -6 to 6
- pair_list: int32 [64, 2], replicated, may hold values from 0 to 127, as said below
- ridge_index: int32 [64], replicated, may hold values from 0 to 3
Outputs:
- predicted: float32 [64, 3, 128, 2, 64], P('snap', None, 'height')
- misfit: float32 [1], replicated
The draws below stay inside these ranges and needn't reach their ends.
Inputs may be any that keep to these rules, and one draw needn't show every extreme that they name: `pair_list`: each row names a streamwise mode below 16 and a spanwise wavenumber below 128; no row repeats.
All inputs are finite; a program needn't handle non-finite values.
Results may differ from the reference program's by a relative error of at most 0.0032.
Values sent between devices are 32-bit elements; how exact they have to be, the bound alone decides.
A program may use at most 128 MiB of HBM per device.

```python
import math
import jax
import jax.numpy as jnp
from jax import lax

Z = 128
KX = 16
H = 128
C = 3
S = 64
PAIRS = 64


def draw_pair_list(key, part):
    total = KX * Z
    first = jax.random.permutation(jax.random.fold_in(key, 11), total - 1)[:PAIRS - 1].astype(jnp.int32)
    chosen = jnp.concatenate([first, jnp.full((1,), total - 1, jnp.int32)])
    order = jax.random.permutation(jax.random.fold_in(key, 12), PAIRS)
    chosen = chosen[order]
    return jnp.stack([chosen // Z, chosen % Z], axis=1).astype(jnp.int32)


def plant(entries, stream_key, least, high):
    place = [jax.random.randint(jax.random.fold_in(stream_key, axis), (), 0, length) for axis, length in enumerate(entries.shape)]
    longest = entries.shape.index(max(entries.shape))
    neighbour = place[:longest] + [(place[longest] + 1) % entries.shape[longest]] + place[longest + 1:]
    return entries.at[tuple(place)].set(least).at[tuple(neighbour)].set(high)


def shard_levels(rng, dims, shards, least, largest):
    def one(position, parts):
        heights = jax.random.uniform(jax.random.fold_in(jax.random.fold_in(rng, 6), position), (parts,), jnp.float32, least / len(shards), largest / len(shards))
        return jnp.repeat(jnp.exp(heights), dims[position] // parts).reshape((-1,) + (1,) * (len(dims) - position - 1))

    level = one(*shards[0])
    for cut in shards[1:]:
        level = level * one(*cut)
    return level


def bell_draw(stream_key, extent, scale, limit, split=(), held_as=jnp.bfloat16):
    level = shard_levels(stream_key, extent, split, -0.22, 0.18) if split else 1.0
    drawn = jax.random.normal(stream_key, extent, jnp.float32) * scale * level
    return jnp.minimum(jnp.maximum(drawn, -limit), limit).astype(held_as)


def setup_inputs(seed: int = 0) -> dict:
    keys = jax.random.split(jax.random.key(seed), 5)
    return {
        "resolved": bell_draw(keys[0], (S, C, H, KX, 2, Z), 1.0, 6.0, ((0, 4), (2, 8))),
        "drain": bell_draw(keys[1], (S, C, H, KX, 2, Z), 1.0, 6.0, ((0, 4), (2, 8))),
        "pair_list": draw_pair_list(jax.random.fold_in(keys[4], 71), 0),
        "ridge_index": plant(jax.random.randint(keys[3], (PAIRS,), 0, 4), jax.random.fold_in(keys[3], 1), 0, 3).astype(jnp.int32),
    }


def twiddles(length):
    grid = jnp.arange(length, dtype=jnp.int32)
    phase = grid[:, None] * grid[None, :] % length
    theta = phase.astype(jnp.float32) * (2.0 * math.pi / length)
    scaling = 1.0 / math.sqrt(length)
    cosine = jnp.cos(theta) * scaling
    sine = jnp.sin(theta) * scaling
    upper = jnp.concatenate([cosine, -sine], axis=1)
    lower = jnp.concatenate([sine, cosine], axis=1)
    return jnp.concatenate([upper, lower], axis=0).astype(jnp.bfloat16)

def spectrum_at(values, entry, twiddle):
    mode_rows = jnp.take(values, entry[0], axis=3)
    picked = jnp.stack([jnp.take(twiddle, entry[1], axis=1), jnp.take(twiddle, entry[1] + Z, axis=1)], axis=1)
    spectral = jnp.dot(mode_rows.reshape(-1, 2 * Z).astype(jnp.float32), picked.astype(jnp.float32), preferred_element_type=jnp.float32)
    return spectral.reshape(S, C * H, 2)

def reference(resolved, drain, pair_list, ridge_index):
    twiddle = twiddles(Z)
    features = C * H
    identity_matrix = jnp.eye(2 * features, dtype=jnp.float32)
    highest = lax.Precision.HIGHEST

    def one_pair(packed):
        entry, level = packed
        ridge = 0.25 * jnp.exp2(level.astype(jnp.float32))
        spec_x = spectrum_at(resolved, entry, twiddle)
        spec_y = spectrum_at(drain, entry, twiddle)
        real_x = spec_x[:, :, 0]
        imag_x = spec_x[:, :, 1]
        stacked_x = jnp.concatenate([jnp.concatenate([real_x, imag_x], 1), jnp.concatenate([-imag_x, real_x], 1)], 0)
        stacked_y = jnp.concatenate([spec_y[:, :, 0], spec_y[:, :, 1]], 0)
        gram = jnp.dot(stacked_x.T.astype(jnp.float32), stacked_x.astype(jnp.float32), precision=highest, preferred_element_type=jnp.float32) / S + ridge * identity_matrix
        moments = jnp.dot(stacked_x.T.astype(jnp.float32), stacked_y.astype(jnp.float32), precision=highest, preferred_element_type=jnp.float32) / S
        factor = jnp.linalg.cholesky(gram)
        halfway = lax.linalg.triangular_solve(factor, moments, left_side=True, lower=True, transpose_a=False)
        weights = lax.linalg.triangular_solve(factor, halfway, left_side=True, lower=True, transpose_a=True)
        fitted = jnp.dot(stacked_x.astype(jnp.float32), weights.astype(jnp.float32), precision=highest, preferred_element_type=jnp.float32)
        misses = jnp.sum((stacked_y - fitted) ** 2)
        energy = jnp.sum(stacked_y ** 2)
        return (fitted.reshape(2, S, C, H), misses, energy)
    fitted_all, misses_all, energy_all = lax.map(one_pair, (pair_list, ridge_index))
    predicted = jnp.transpose(fitted_all, (2, 3, 4, 1, 0))
    misfit = (jnp.sum(misses_all) / jnp.sum(energy_all)).reshape(1)
    return (predicted, misfit)
```

```python
import functools
import math

import jax
import jax.numpy as jnp
import numpy as np
from jax import lax
from jax.experimental import pallas as pl
from jax.experimental.pallas import tpu as pltpu
from jax.sharding import PartitionSpec as P

HIGHEST = lax.Precision.HIGHEST
LANES = 128
TILE = 8
VMEM_BYTES = 48 << 20


def wave_table(points):
    grid = np.arange(points)
    theta = (grid[:, None] * grid[None, :] % points).astype(np.float32) * np.float32(2.0 * math.pi / points)
    scaling = np.float32(1.0 / math.sqrt(points))
    cosine = (np.cos(theta) * scaling).T
    sine = (np.sin(theta) * scaling).T
    rows = np.concatenate([np.concatenate([cosine, sine], 1), np.concatenate([-sine, cosine], 1)], 0)
    return rows.astype(jnp.bfloat16)


def round_up(value, unit):
    return -(-value // unit) * unit


def swap_groups(arrays, width):
    arrays = list(arrays)
    lane = lax.broadcasted_iota(jnp.int32, (1, LANES), 1)
    bit = 1
    while bit < len(arrays):
        low = (lane // width) % (2 * bit) < bit
        for index in range(len(arrays)):
            if index & bit:
                continue
            first, second = arrays[index], arrays[index + bit]
            arrays[index] = jnp.where(low, first, pltpu.roll(second, bit * width, 1))
            arrays[index + bit] = jnp.where(low, pltpu.roll(first, LANES - bit * width, 1), second)
        bit *= 2
    return arrays


def invert(gram, ridge):
    pairs = len(gram)
    snaps = gram[0].shape[0] // 2
    lane = lax.broadcasted_iota(jnp.int32, (snaps, 2 * snaps), 1)
    line = lax.broadcasted_iota(jnp.int32, (snaps, 2 * snaps), 0)
    sign = jnp.where(lax.broadcasted_iota(jnp.int32, (1, 2 * snaps), 1) < snaps, -1.0, 1.0)
    grams = []
    states = []
    for pair in range(pairs):
        whole = gram[pair]
        swapped = pltpu.roll(whole[snaps:], snaps, 1)
        top = whole[:snaps] + jnp.where(lane < snaps, swapped, 0.0)
        top = jnp.where(lane < snaps, top, swapped - whole[:snaps])
        grams.append(top)
        states.append(top + jnp.where(line == lane, ridge[pair], 0.0))
    turned = [pltpu.roll(state, snaps, 1) * sign for state in states]
    for k in range(snaps):
        here = line == k
        column = (lane == k) | (lane == snaps + k)
        unit = jnp.where(here & (lane == k), 1.0, 0.0)
        other = jnp.where(here & (lane == snaps + k), 1.0, 0.0)
        for pair in range(pairs):
            state, twin = states[pair], turned[pair]
            first = state[:, k:k + 1]
            second = state[:, snaps + k:snaps + k + 1]
            inverse = 1.0 / state[k:k + 1, k:k + 1]
            cleared = jnp.where(column, unit, state)
            cleared_twin = jnp.where(column, other, twin)
            row = cleared[k:k + 1, :] * inverse
            row_twin = cleared_twin[k:k + 1, :] * inverse
            states[pair] = jnp.where(here, row, cleared - (first * row + second * row_twin))
            turned[pair] = jnp.where(here, row_twin, cleared_twin - (first * row_twin - second * row))
    smooth = []
    for pair in range(pairs):
        full = jnp.concatenate([grams[pair], pltpu.roll(grams[pair], snaps, 1) * sign], axis=0)
        smooth.append(jnp.dot(full, jnp.concatenate([states[pair], turned[pair]], axis=0), precision=HIGHEST,
                              preferred_element_type=jnp.float32))
    return smooth


class Sizes:
    def __init__(self, shape, pair_total, snap_count, height_count):
        self.snap_local, self.components, self.height_local, self.modes, self.parts, self.points = shape
        self.snap_count, self.height_count = snap_count, height_count
        self.owners = snap_count * height_count
        self.pairs = pair_total
        self.pair_local = pair_total // self.owners
        self.near = self.components * self.height_local
        self.snaps = snap_count * self.snap_local
        self.groups = LANES // self.snap_local
        self.tiles = self.near // self.groups
        self.tiles_each = self.height_local // self.groups
        self.columns = 2 * self.pairs
        self.kinds = 2 * self.pair_local
        self.sent = self.tiles * self.kinds
        self.out_stride = round_up(self.sent, TILE)
        self.back = self.sent + 1
        self.back_stride = round_up(self.back, TILE)
        self.wide = self.modes * self.parts * self.points


def whole_kernel(z, wave_hbm, list_ref, ridge_ref, x_hbm, y_hbm, predicted_ref, misfit_ref,
                 wave, x_buf, y_buf, table, x_out, y_out, x_in, y_in, x_rows, y_rows, b_out, b_in,
                 load_sem, x_send, x_recv, y_send, y_recv, b_send, b_recv, own_sem):
    me = lax.axis_index("snap") * z.height_count + lax.axis_index("height")
    barrier = pltpu.get_barrier_semaphore()

    def peer(step):
        other = lax.rem(me + step, z.owners)
        return other, (other // z.height_count, lax.rem(other, z.height_count))

    def load(source, target, part, index):
        span = pl.ds(part * z.height_local, z.height_local)
        return pltpu.make_async_copy(source.at[:, span], target.at[:, span], load_sem.at[index])

    wave_copy = pltpu.make_async_copy(wave_hbm, wave, load_sem.at[0])
    wave_copy.start()
    x_loads = [load(x_hbm, x_buf, part, 1 + part) for part in range(z.components)]
    y_loads = [load(y_hbm, y_buf, part, 1 + z.components + part) for part in range(z.components)]
    for item in x_loads + y_loads:
        item.start()

    def greet(step, carry):
        _, where = peer(step)
        pl.semaphore_signal(barrier, inc=1, device_id=where, device_id_type=pl.DeviceIdType.MESH)
        return carry

    lax.fori_loop(1, z.owners, greet, 0)

    same = (lax.broadcasted_iota(jnp.int32, (z.pairs, z.pairs), 0)
            == lax.broadcasted_iota(jnp.int32, (z.pairs, z.pairs), 1))
    mode = jnp.sum(jnp.where(same, list_ref[0:1, :], 0), axis=1, keepdims=True)
    number = jnp.sum(jnp.where(same, list_ref[1:2, :], 0), axis=1, keepdims=True)
    mode = jnp.concatenate([mode, mode], axis=0)
    number = jnp.concatenate([number, number + z.points], axis=0)
    chosen = lax.broadcasted_iota(jnp.int32, (z.columns, 2 * z.points), 1) == number
    wave_copy.wait()
    picked = jnp.dot(jnp.where(chosen, 1.0, 0.0).astype(jnp.bfloat16), wave[...], preferred_element_type=jnp.float32)
    for index in range(z.modes):
        table[:, index * 2 * z.points:(index + 1) * 2 * z.points] = jnp.where(mode == index, picked, 0.0).astype(jnp.bfloat16)
    x_rows[...] = jnp.zeros_like(x_rows)
    y_rows[...] = jnp.zeros_like(y_rows)

    def spectrum(buf, loads, out):
        for part in range(z.components):
            loads[part].wait()
            rows = jnp.concatenate([buf[:, part * z.height_local + height].reshape(z.snap_local, z.wide)
                                    for height in range(z.height_local)], axis=0)
            product = lax.dot_general(table[...], rows, (((1,), (1,)), ((), ())), preferred_element_type=jnp.float32)
            for each in range(z.tiles_each):
                tile = part * z.tiles_each + each
                for kind in range(z.kinds):
                    out[pl.ds(tile * z.kinds + kind, z.owners, stride=z.out_stride), :] = (
                        product[kind * z.owners:(kind + 1) * z.owners, each * LANES:(each + 1) * LANES])

    def exchange(source, target, rows, stride, send, recv, own):
        def here(index):
            return pl.ds(pl.multiple_of(index * stride, TILE), rows)

        def copy(step):
            other, where = peer(step)
            return pltpu.make_async_remote_copy(
                src_ref=source.at[here(other)], dst_ref=target.at[here(me)], send_sem=send.at[step], recv_sem=recv.at[step],
                device_id=where, device_id_type=pl.DeviceIdType.MESH)

        kept = pltpu.make_async_copy(source.at[here(me)], target.at[here(me)], own_sem.at[own])

        def start():
            def one(step, carry):
                copy(step).start()
                return carry
            kept.start()
            lax.fori_loop(1, z.owners, one, 0)

        def finish():
            def one(step, carry):
                copy(step).wait()
                return carry
            lax.fori_loop(1, z.owners, one, 0)
            kept.wait()

        return start, finish

    x_start, x_finish = exchange(x_out, x_in, z.sent, z.out_stride, x_send, x_recv, 0)
    y_start, y_finish = exchange(y_out, y_in, z.sent, z.out_stride, y_send, y_recv, 1)
    b_start, b_finish = exchange(b_out, b_in, z.back, z.back_stride, b_send, b_recv, 2)

    spectrum(x_buf, x_loads, x_out)
    pl.semaphore_wait(barrier, z.owners - 1)
    x_start()
    spectrum(y_buf, y_loads, y_out)
    y_start()
    x_finish()

    sets = 2 * z.snap_count // z.groups

    def place(pair, height, index, stride):
        half, snap = index // z.snap_count, index % z.snap_count
        start = (snap * z.height_count + height) * stride + half * z.pair_local + pair
        return pl.ds(start, z.tiles, stride=z.kinds)

    def gather(source, target, pair):
        for height in range(z.height_count):
            for part in range(sets):
                moved = swap_groups([source[place(pair, height, part * z.groups + index, z.out_stride), :]
                                     for index in range(z.groups)], z.snap_local)
                for index, piece in enumerate(moved):
                    target[pair, pl.ds((height * z.groups + index) * TILE, z.tiles), part * LANES:(part + 1) * LANES] = piece

    gram = []
    ridge = []
    for pair in range(z.pair_local):
        gather(x_in, x_rows, pair)
        rows = x_rows[pair]
        gram.append(lax.dot_general(rows, rows, (((0,), (0,)), ((), ())), precision=HIGHEST, preferred_element_type=jnp.float32))
        mine = lax.broadcasted_iota(jnp.int32, (1, z.pairs), 1) == pair * z.owners + me
        level = jnp.sum(jnp.where(mine, ridge_ref[...], 0), axis=1, keepdims=True)
        ridge.append(lax.shift_left(jnp.ones_like(level), level).astype(jnp.float32) * (0.25 * z.snaps))
    smooth = invert(gram, ridge)

    y_finish()
    misses = jnp.zeros((1, 1), jnp.float32)
    energy = jnp.zeros((1, 1), jnp.float32)
    for pair in range(z.pair_local):
        gather(y_in, y_rows, pair)
        target = y_rows[pair]
        fitted = lax.dot_general(target, smooth[pair], (((1,), (1,)), ((), ())), precision=HIGHEST,
                                 preferred_element_type=jnp.float32)
        gap = target - fitted
        misses = misses + jnp.sum(gap * gap, keepdims=True)
        energy = energy + jnp.sum(target * target, keepdims=True)
        for height in range(z.height_count):
            for part in range(sets):
                moved = swap_groups([fitted[(height * z.groups + index) * TILE:(height * z.groups + index + 1) * TILE,
                                            part * LANES:(part + 1) * LANES] for index in range(z.groups)], z.snap_local)
                for index, piece in enumerate(moved):
                    b_out[place(pair, height, part * z.groups + index, z.back_stride), :] = piece[:z.tiles]
    lane = lax.broadcasted_iota(jnp.int32, (1, LANES), 1)
    note = jnp.where(lane == 0, misses, jnp.where(lane == 1, energy, 0.0))
    b_out[pl.ds(z.sent, z.owners, stride=z.back_stride), :] = jnp.broadcast_to(note, (z.owners, LANES))
    b_start()
    b_finish()

    for tile in range(z.tiles):
        for half in range(2):
            sheet = jnp.concatenate([b_in[pl.ds(tile * z.kinds + half * z.pair_local + pair, z.owners, stride=z.back_stride), :]
                                     for pair in range(z.pair_local)], axis=0)
            turned = sheet.T
            for index in range(z.groups):
                first = (tile * z.groups + index) * 2 + half
                block = turned[index * z.snap_local:(index + 1) * z.snap_local]
                if z.pairs <= LANES:
                    predicted_ref[pl.ds(first, z.snap_local, stride=2 * z.near), :] = block
                else:
                    for snap in range(z.snap_local):
                        predicted_ref[pl.ds(first + snap * 2 * z.near, 1), :] = block[snap:snap + 1]
    notes = jnp.sum(b_in[pl.ds(z.sent, z.owners, stride=z.back_stride), :], axis=0, keepdims=True)
    misfit_ref[...] = notes[:, 0:1] / notes[:, 1:2]


def per_device(resolved, drain, pair_list, ridge_index):
    z = Sizes(resolved.shape, pair_list.shape[0], lax.axis_size("snap"), lax.axis_size("height"))
    vmem = pl.BlockSpec(memory_space=pltpu.VMEM)
    hbm = pl.BlockSpec(memory_space=pltpu.HBM)
    block = (z.snap_local, z.near, z.modes * z.parts, z.points)
    out_rows = z.owners * z.out_stride
    back_rows = z.owners * z.back_stride
    gathered = (z.pair_local, z.height_count * z.groups * TILE, 2 * z.snaps)
    dma = pltpu.SemaphoreType.DMA((z.owners,))
    predicted, misfit = pl.pallas_call(
        functools.partial(whole_kernel, z),
        in_specs=[hbm, vmem, vmem, hbm, hbm],
        out_specs=[vmem, vmem],
        out_shape=[jax.ShapeDtypeStruct((z.snap_local * z.near * 2, z.pairs), jnp.float32),
                   jax.ShapeDtypeStruct((1, 1), jnp.float32)],
        scratch_shapes=[
            pltpu.VMEM((2 * z.points, 2 * z.points), jnp.bfloat16),
            pltpu.VMEM(block, jnp.bfloat16),
            pltpu.VMEM(block, jnp.bfloat16),
            pltpu.VMEM((z.columns, z.wide), jnp.bfloat16),
            pltpu.VMEM((out_rows, LANES), jnp.float32),
            pltpu.VMEM((out_rows, LANES), jnp.float32),
            pltpu.VMEM((out_rows, LANES), jnp.float32),
            pltpu.VMEM((out_rows, LANES), jnp.float32),
            pltpu.VMEM(gathered, jnp.float32),
            pltpu.VMEM(gathered, jnp.float32),
            pltpu.VMEM((back_rows, LANES), jnp.float32),
            pltpu.VMEM((back_rows, LANES), jnp.float32),
            pltpu.SemaphoreType.DMA((1 + 2 * z.components,)),
            dma, dma, dma, dma, dma, dma,
            pltpu.SemaphoreType.DMA((3,)),
        ],
        compiler_params=pltpu.CompilerParams(collective_id=0, has_side_effects=True, vmem_limit_bytes=VMEM_BYTES),
    )(jnp.asarray(wave_table(z.points)), pair_list.T, ridge_index.reshape(1, z.pairs), resolved.reshape(block), drain.reshape(block))
    predicted = predicted.reshape(z.snap_local, z.components, z.height_local, 2, z.pairs)
    return (predicted, misfit.reshape(1))


def solution(mesh):
    return jax.shard_map(
        per_device,
        mesh=mesh,
        in_specs=(
            P("snap", None, "height", None, None, None),
            P("snap", None, "height", None, None, None),
            P(),
            P(),
        ),
        out_specs=(P("snap", None, "height", None, None), P()),
        check_vma=False,
    )
```

```python
import functools
import math

import jax
import jax.numpy as jnp
import numpy as np
from jax import lax
from jax.experimental import pallas as pl
from jax.experimental.pallas import tpu as pltpu
from jax.sharding import PartitionSpec as P

HIGHEST = lax.Precision.HIGHEST
LANES = 128
TILE = 8
VMEM_BYTES = 48 << 20


def wave_table(points):
    grid = np.arange(points)
    theta = (grid[:, None] * grid[None, :] % points).astype(np.float32) * np.float32(2.0 * math.pi / points)
    scaling = np.float32(1.0 / math.sqrt(points))
    cosine = (np.cos(theta) * scaling).T
    sine = (np.sin(theta) * scaling).T
    rows = np.concatenate([np.concatenate([cosine, sine], 1), np.concatenate([-sine, cosine], 1)], 0)
    return rows.astype(jnp.bfloat16)


def round_up(value, unit):
    return -(-value // unit) * unit


def swap_groups(arrays, width):
    arrays = list(arrays)
    lane = lax.broadcasted_iota(jnp.int32, (1, LANES), 1)
    bit = 1
    while bit < len(arrays):
        low = (lane // width) % (2 * bit) < bit
        for index in range(len(arrays)):
            if index & bit:
                continue
            first, second = arrays[index], arrays[index + bit]
            arrays[index] = jnp.where(low, first, pltpu.roll(second, bit * width, 1))
            arrays[index + bit] = jnp.where(low, pltpu.roll(first, LANES - bit * width, 1), second)
        bit *= 2
    return arrays


def invert(gram, ridge):
    pairs = len(gram)
    snaps = gram[0].shape[0] // 2
    lane = lax.broadcasted_iota(jnp.int32, (snaps, 2 * snaps), 1)
    line = lax.broadcasted_iota(jnp.int32, (snaps, 2 * snaps), 0)
    sign = jnp.where(lax.broadcasted_iota(jnp.int32, (1, 2 * snaps), 1) < snaps, -1.0, 1.0)
    grams = []
    states = []
    for pair in range(pairs):
        whole = gram[pair]
        swapped = pltpu.roll(whole[snaps:], snaps, 1)
        top = whole[:snaps] + jnp.where(lane < snaps, swapped, 0.0)
        top = jnp.where(lane < snaps, top, swapped - whole[:snaps])
        grams.append(top)
        states.append(top + jnp.where(line == lane, ridge[pair], 0.0))
    turned = [pltpu.roll(state, snaps, 1) * sign for state in states]
    for k in range(0, snaps, 2):
        near, far = line == k, line == k + 1
        column = (lane // 2 == k // 2) | (lane // 2 == (snaps + k) // 2)
        unit = jnp.where((near | far) & (lane == line), 1.0, 0.0)
        other = jnp.where((near | far) & (lane == snaps + line), 1.0, 0.0)
        for pair in range(pairs):
            state, twin = states[pair], turned[pair]
            first_re, second_re = state[:, k:k + 1], state[:, k + 1:k + 2]
            first_im, second_im = state[:, snaps + k:snaps + k + 1], state[:, snaps + k + 1:snaps + k + 2]
            head, tail = state[k:k + 1, k:k + 1], state[k + 1:k + 2, k + 1:k + 2]
            cross_re, cross_im = state[k:k + 1, k + 1:k + 2], state[k:k + 1, snaps + k + 1:snaps + k + 2]
            inverse = 1.0 / (head * tail - (cross_re * cross_re + cross_im * cross_im))
            head, tail, cross_re, cross_im = head * inverse, tail * inverse, cross_re * inverse, cross_im * inverse
            cleared = jnp.where(column, unit, state)
            cleared_twin = jnp.where(column, other, twin)
            one, two = cleared[k:k + 1, :], cleared[k + 1:k + 2, :]
            one_twin, two_twin = cleared_twin[k:k + 1, :], cleared_twin[k + 1:k + 2, :]
            top = tail * one - (cross_re * two + cross_im * two_twin)
            top_twin = tail * one_twin - (cross_re * two_twin - cross_im * two)
            low = head * two - (cross_re * one - cross_im * one_twin)
            low_twin = head * two_twin - (cross_re * one_twin + cross_im * one)
            fresh = cleared - ((first_re * top + first_im * top_twin) + (second_re * low + second_im * low_twin))
            fresh_twin = cleared_twin - ((first_re * top_twin - first_im * top) + (second_re * low_twin - second_im * low))
            states[pair] = jnp.where(near, top, jnp.where(far, low, fresh))
            turned[pair] = jnp.where(near, top_twin, jnp.where(far, low_twin, fresh_twin))
    return [jnp.dot(grams[pair], jnp.concatenate([states[pair], turned[pair]], axis=0), precision=HIGHEST,
                    preferred_element_type=jnp.float32) for pair in range(pairs)]


class Sizes:
    def __init__(self, shape, pair_total, snap_count, height_count):
        self.snap_local, self.components, self.height_local, self.modes, self.parts, self.points = shape
        self.snap_count, self.height_count = snap_count, height_count
        self.owners = snap_count * height_count
        self.pairs = pair_total
        self.pair_local = pair_total // self.owners
        self.near = self.components * self.height_local
        self.snaps = snap_count * self.snap_local
        self.groups = LANES // self.snap_local
        self.tiles = self.near // self.groups
        self.tiles_each = self.height_local // self.groups
        self.columns = 2 * self.pairs
        self.kinds = 2 * self.pair_local
        self.sent = self.tiles * self.kinds
        self.out_stride = round_up(self.sent, TILE)
        self.back = self.sent + 1
        self.back_stride = round_up(self.back, TILE)
        self.wide = self.modes * self.parts * self.points
        self.half_heights = height_count // 2
        self.half_owners = snap_count * self.half_heights
        self.sets = 2 * snap_count // self.groups


def embed(top):
    snaps = top.shape[0]
    sign = jnp.where(lax.broadcasted_iota(jnp.int32, (1, 2 * snaps), 1) < snaps, -1.0, 1.0)
    return jnp.concatenate([top, pltpu.roll(top, snaps, 1) * sign], axis=0)


def whole_kernel(z, wave_hbm, list_hbm, ridge_hbm, x_hbm, y_hbm, predicted_ref, misfit_ref,
                 wave, list_ref, ridge_ref, x_buf, y_buf, table, x_out, y_out, x_in, y_in, x_rows, y_rows, s_out, s_in,
                 b_out, b_in, note_out, note_in,
                 load_sem, x_send, x_recv, y_send, y_recv, s_send, s_recv, b_send, b_recv, note_send, note_recv, own_sem):
    snap, height = lax.axis_index("snap"), lax.axis_index("height")
    half, inner = height // z.half_heights, lax.rem(height, z.half_heights)
    own_slot = snap * z.height_count + inner * 2 + half
    twin_slot = snap * z.height_count + inner * 2 + (1 - half)
    barrier = pltpu.get_barrier_semaphore()

    def wrap(value, count):
        return lax.rem(value + count, count)

    def slot_of(snap_at, height_at):
        return snap_at * z.height_count + lax.rem(height_at, z.half_heights) * 2 + height_at // z.half_heights

    def away(step):
        return wrap(snap + lax.rem(step, z.snap_count), z.snap_count), wrap(height + step // z.snap_count, z.height_count)

    def beside(step, sign, side):
        return (wrap(snap + sign * lax.rem(step, z.snap_count), z.snap_count),
                side * z.half_heights + wrap(inner + sign * (step // z.snap_count), z.half_heights))

    def load(source, target, part, index):
        span = pl.ds(part * z.height_local, z.height_local)
        return pltpu.make_async_copy(source.at[:, span], target.at[:, span], load_sem.at[index])

    small = [pltpu.make_async_copy(source, target, load_sem.at[2 * z.components + index])
             for index, (source, target) in enumerate([(list_hbm, list_ref), (wave_hbm, wave), (ridge_hbm, ridge_ref)])]
    for item in small:
        item.start()
    x_loads = [load(x_hbm, x_buf, part, part) for part in range(z.components)]
    y_loads = [load(y_hbm, y_buf, part, z.components + part) for part in range(z.components)]
    for item in x_loads + y_loads:
        item.start()

    def greet(step, carry):
        pl.semaphore_signal(barrier, inc=1, device_id=away(step), device_id_type=pl.DeviceIdType.MESH)
        return carry

    lax.fori_loop(1, z.owners, greet, 0)

    same = (lax.broadcasted_iota(jnp.int32, (z.pairs, z.pairs), 0)
            == lax.broadcasted_iota(jnp.int32, (z.pairs, z.pairs), 1))
    small[0].wait()
    mode = jnp.sum(jnp.where(same, list_ref[0:1, :], 0), axis=1, keepdims=True)
    number = jnp.sum(jnp.where(same, list_ref[1:2, :], 0), axis=1, keepdims=True)
    mode = jnp.concatenate([mode, mode], axis=0)
    number = jnp.concatenate([number, number + z.points], axis=0)
    chosen = lax.broadcasted_iota(jnp.int32, (z.columns, 2 * z.points), 1) == number
    small[1].wait()
    picked = jnp.dot(jnp.where(chosen, 1.0, 0.0).astype(jnp.bfloat16), wave[...], preferred_element_type=jnp.float32)
    for index in range(z.modes):
        table[:, index * 2 * z.points:(index + 1) * 2 * z.points] = jnp.where(mode == index, picked, 0.0).astype(jnp.bfloat16)
    x_rows[...] = jnp.zeros_like(x_rows)
    y_rows[...] = jnp.zeros_like(y_rows)

    def spectrum(buf, loads, out):
        for part in range(z.components):
            loads[part].wait()
            rows = jnp.concatenate([buf[:, part * z.height_local + index].reshape(z.snap_local, z.wide)
                                    for index in range(z.height_local)], axis=0)
            product = lax.dot_general(table[...], rows, (((1,), (1,)), ((), ())), preferred_element_type=jnp.float32)
            for each in range(z.tiles_each):
                tile = part * z.tiles_each + each
                for kind in range(z.kinds):
                    out[pl.ds(tile * z.kinds + kind, z.owners, stride=z.out_stride), :] = (
                        product[kind * z.owners:(kind + 1) * z.owners, each * LANES:(each + 1) * LANES])

    def at(index, stride, rows):
        return pl.ds(pl.multiple_of(index * stride, TILE), rows)

    def remote(source, target, send, recv, where):
        return pltpu.make_async_remote_copy(src_ref=source, dst_ref=target, send_sem=send, recv_sem=recv, device_id=where,
                                            device_id_type=pl.DeviceIdType.MESH)

    def each(copy, first, last, act):
        def one(step, carry):
            act(copy(step))
            return carry
        lax.fori_loop(first, last, one, 0)

    def start(item):
        item.start()

    def sent(item):
        item.wait_send()

    def arrived(item):
        item.wait_recv()

    def x_copy(step):
        where = away(step)
        return remote(x_out.at[at(slot_of(*where), z.out_stride, z.sent)], x_in.at[at(step, z.out_stride, z.sent)],
                      x_send.at[step], x_recv.at[step], where)

    def y_copy(step):
        where = beside(step, 1, half)
        first = where[0] * z.height_count + lax.rem(where[1], z.half_heights) * 2
        return remote(y_out.at[at(first, z.out_stride, 2 * z.out_stride)], y_in.at[at(step, 2 * z.out_stride, 2 * z.out_stride)],
                      y_send.at[step], y_recv.at[step], where)

    def b_copy(side, target):
        def copy(step):
            return remote(b_out.at[side, at(step, z.back_stride, z.back)], b_in.at[at(target, z.back_stride, z.back)],
                          b_send.at[side, step], b_recv.at[side, step], beside(step, -1, half))
        return copy

    def note_copy(step):
        return remote(note_out.at[pl.ds(0, 1)], note_in.at[at(step, TILE, 1)], note_send.at[step], note_recv.at[step],
                      beside(step, 1, 1 - half))

    x_kept = pltpu.make_async_copy(x_out.at[at(own_slot, z.out_stride, z.sent)], x_in.at[at(0, z.out_stride, z.sent)], own_sem.at[0])
    y_kept = pltpu.make_async_copy(
        y_out.at[at(snap * z.height_count + inner * 2, z.out_stride, 2 * z.out_stride)],
        y_in.at[at(0, 2 * z.out_stride, 2 * z.out_stride)], own_sem.at[1])
    slots = (own_slot, twin_slot)
    b_kept = [pltpu.make_async_copy(b_out.at[side, at(0, z.back_stride, z.back)], b_in.at[at(slots[side], z.back_stride, z.back)],
                                    own_sem.at[2 + side]) for side in range(2)]
    s_copy = remote(s_out, s_in, s_send, s_recv, (snap, (1 - half) * z.half_heights + inner))

    spectrum(x_buf, x_loads, x_out)
    pl.semaphore_wait(barrier, z.owners - 1)
    x_kept.start()
    each(x_copy, 1, z.owners, start)
    spectrum(y_buf, y_loads, y_out)
    y_kept.start()
    each(y_copy, 1, z.half_owners, start)

    def place(base, index, pair):
        part, member = index // z.snap_count, index % z.snap_count
        return base(member) + part * z.pair_local + pair

    def gather(source, base, pair, target, block):
        for group in range(z.sets):
            moved = swap_groups([source[pl.ds(place(base, group * z.groups + index, pair), z.tiles, stride=z.kinds), :]
                                 for index in range(z.groups)], z.snap_local)
            for index, piece in enumerate(moved):
                target[pl.ds((block * z.groups + index) * TILE, z.tiles), group * LANES:(group + 1) * LANES] = piece

    gram = [None] * z.pair_local
    batch = min(4, z.height_count)
    span = batch * z.groups * TILE
    for block in range(z.height_count):
        for member in range(z.snap_count):
            step = block * z.snap_count + member
            if step == 0:
                x_kept.wait()
            else:
                x_copy(step).wait_recv()
        for pair in range(z.pair_local):
            gather(x_in, lambda member: (block * z.snap_count + member) * z.out_stride, pair, x_rows.at[pair], block)
            if block % batch == batch - 1:
                rows = x_rows[pair, pl.ds((block // batch) * span, span), :]
                term = lax.dot_general(rows, rows, (((0,), (0,)), ((), ())), precision=HIGHEST, preferred_element_type=jnp.float32)
                gram[pair] = term if gram[pair] is None else gram[pair] + term
    small[2].wait()
    ridge = []
    for pair in range(z.pair_local):
        mine = lax.broadcasted_iota(jnp.int32, (1, z.pairs), 1) == pair * z.owners + own_slot
        level = jnp.sum(jnp.where(mine, ridge_ref[...], 0), axis=1, keepdims=True)
        ridge.append(lax.shift_left(jnp.ones_like(level), level).astype(jnp.float32) * (0.25 * z.snaps))
    tops = invert(gram, ridge)
    for pair in range(z.pair_local):
        s_out[pair] = tops[pair]
    s_copy.start()

    y_kept.wait()
    each(y_copy, 1, z.half_owners, arrived)
    lane = lax.broadcasted_iota(jnp.int32, (1, LANES), 1)

    def collect(side):
        which = half if side == 0 else 1 - half
        for pair in range(z.pair_local):
            for block in range(z.half_heights):
                gather(y_in, lambda member: ((block * z.snap_count + member) * 2 + which) * z.out_stride, pair,
                       y_rows.at[side, pair], block)

    def fit(side, tops):
        misses = jnp.zeros((1, 1), jnp.float32)
        energy = jnp.zeros((1, 1), jnp.float32)
        for pair in range(z.pair_local):
            target = y_rows[side, pair]
            fitted = lax.dot_general(target, embed(tops[pair]), (((1,), (1,)), ((), ())), precision=HIGHEST,
                                     preferred_element_type=jnp.float32)
            gap = target - fitted
            misses = misses + jnp.sum(gap * gap, keepdims=True)
            energy = energy + jnp.sum(target * target, keepdims=True)
            for block in range(z.half_heights):
                for group in range(z.sets):
                    moved = swap_groups([fitted[(block * z.groups + index) * TILE:(block * z.groups + index + 1) * TILE,
                                                group * LANES:(group + 1) * LANES] for index in range(z.groups)], z.snap_local)
                    for index, piece in enumerate(moved):
                        row = place(lambda member: (block * z.snap_count + member) * z.back_stride, group * z.groups + index, pair)
                        b_out[side, pl.ds(row, z.tiles, stride=z.kinds), :] = piece[:z.tiles]
        note = jnp.where(lane == 0, misses, jnp.where(lane == 1, energy, 0.0))
        for step in range(z.half_owners):
            b_out[side, pl.ds(step * z.back_stride + z.sent, 1), :] = note
        return note

    collect(0)
    note = fit(0, tops)
    b_kept[0].start()
    each(b_copy(0, own_slot), 1, z.half_owners, start)
    collect(1)
    s_copy.wait_recv()
    note = note + fit(1, [s_in[pair] for pair in range(z.pair_local)])
    b_kept[1].start()
    each(b_copy(1, twin_slot), 1, z.half_owners, start)
    note_out[...] = jnp.broadcast_to(note, note_out.shape)
    each(note_copy, 0, z.half_owners, start)

    each(x_copy, 1, z.owners, sent)
    each(y_copy, 1, z.half_owners, sent)
    s_copy.wait_send()
    for side in range(2):
        b_kept[side].wait()
        each(b_copy(side, slots[side]), 1, z.half_owners, arrived)
    each(note_copy, 0, z.half_owners, arrived)

    for tile in range(z.tiles):
        for part in range(2):
            sheet = jnp.concatenate([b_in[pl.ds(tile * z.kinds + part * z.pair_local + pair, z.owners, stride=z.back_stride), :]
                                     for pair in range(z.pair_local)], axis=0)
            turned = sheet.T
            for index in range(z.groups):
                first = (tile * z.groups + index) * 2 + part
                piece = turned[index * z.snap_local:(index + 1) * z.snap_local]
                if z.pairs <= LANES:
                    predicted_ref[pl.ds(first, z.snap_local, stride=2 * z.near), :] = piece
                else:
                    for line in range(z.snap_local):
                        predicted_ref[pl.ds(first + line * 2 * z.near, 1), :] = piece[line:line + 1]
    notes = (jnp.sum(b_in[pl.ds(z.sent, z.owners, stride=z.back_stride), :], axis=0, keepdims=True)
             + jnp.sum(note_in[pl.ds(0, z.half_owners, stride=TILE), :], axis=0, keepdims=True))
    misfit_ref[...] = notes[:, 0:1] / notes[:, 1:2]
    for side in range(2):
        each(b_copy(side, slots[side]), 1, z.half_owners, sent)
    each(note_copy, 0, z.half_owners, sent)


def per_device(resolved, drain, pair_list, ridge_index):
    z = Sizes(resolved.shape, pair_list.shape[0], lax.axis_size("snap"), lax.axis_size("height"))
    vmem = pl.BlockSpec(memory_space=pltpu.VMEM)
    hbm = pl.BlockSpec(memory_space=pltpu.HBM)
    block = (z.snap_local, z.near, z.modes * z.parts, z.points)
    out_rows = z.owners * z.out_stride
    back_rows = z.half_owners * z.back_stride
    gathered = z.groups * TILE
    dma = pltpu.SemaphoreType.DMA
    stay = functools.partial(pltpu.with_memory_space_constraint, memory_space=pltpu.HBM)
    predicted, misfit = pl.pallas_call(
        functools.partial(whole_kernel, z),
        in_specs=[hbm] * 5,
        out_specs=[vmem, vmem],
        out_shape=[jax.ShapeDtypeStruct((z.snap_local * z.near * 2, z.pairs), jnp.float32),
                   jax.ShapeDtypeStruct((1, 1), jnp.float32)],
        scratch_shapes=[
            pltpu.VMEM((2 * z.points, 2 * z.points), jnp.bfloat16),
            pltpu.VMEM((2, z.pairs), jnp.int32),
            pltpu.VMEM((1, z.pairs), jnp.int32),
            pltpu.VMEM(block, jnp.bfloat16),
            pltpu.VMEM(block, jnp.bfloat16),
            pltpu.VMEM((z.columns, z.wide), jnp.bfloat16),
            pltpu.VMEM((out_rows, LANES), jnp.float32),
            pltpu.VMEM((out_rows, LANES), jnp.float32),
            pltpu.VMEM((out_rows, LANES), jnp.float32),
            pltpu.VMEM((out_rows, LANES), jnp.float32),
            pltpu.VMEM((z.pair_local, z.height_count * gathered, 2 * z.snaps), jnp.float32),
            pltpu.VMEM((2, z.pair_local, z.half_heights * gathered, 2 * z.snaps), jnp.float32),
            pltpu.VMEM((z.pair_local, z.snaps, 2 * z.snaps), jnp.float32),
            pltpu.VMEM((z.pair_local, z.snaps, 2 * z.snaps), jnp.float32),
            pltpu.VMEM((2, back_rows, LANES), jnp.float32),
            pltpu.VMEM((2 * back_rows, LANES), jnp.float32),
            pltpu.VMEM((TILE, LANES), jnp.float32),
            pltpu.VMEM((z.half_owners * TILE, LANES), jnp.float32),
            dma((2 * z.components + 3,)),
            dma((z.owners,)), dma((z.owners,)),
            dma((z.half_owners,)), dma((z.half_owners,)),
            dma, dma,
            dma((2, z.half_owners)), dma((2, z.half_owners)),
            dma((z.half_owners,)), dma((z.half_owners,)),
            dma((4,)),
        ],
        compiler_params=pltpu.CompilerParams(collective_id=0, has_side_effects=True, vmem_limit_bytes=VMEM_BYTES),
    )(stay(jnp.asarray(wave_table(z.points))), stay(pair_list.T), stay(ridge_index.reshape(1, z.pairs)),
      resolved.reshape(block), drain.reshape(block))
    predicted = predicted.reshape(z.snap_local, z.components, z.height_local, 2, z.pairs)
    return (predicted, misfit.reshape(1))


def solution(mesh):
    return jax.shard_map(
        per_device,
        mesh=mesh,
        in_specs=(
            P("snap", None, "height", None, None, None),
            P("snap", None, "height", None, None, None),
            P(),
            P(),
        ),
        out_specs=(P("snap", None, "height", None, None), P()),
        check_vma=False,
    )
```

```python
import functools
import math

import jax
import jax.numpy as jnp
import numpy as np
from jax import lax
from jax.experimental import pallas as pl
from jax.experimental.pallas import tpu as pltpu
from jax.sharding import PartitionSpec as P

HIGHEST = lax.Precision.HIGHEST
LANES = 128
TILE = 8
VMEM_BYTES = 48 << 20


def wave_table(points):
    grid = np.arange(points)
    theta = (grid[:, None] * grid[None, :] % points).astype(np.float32) * np.float32(2.0 * math.pi / points)
    scaling = np.float32(1.0 / math.sqrt(points))
    cosine = (np.cos(theta) * scaling).T
    sine = (np.sin(theta) * scaling).T
    rows = np.concatenate([np.concatenate([cosine, sine], 1), np.concatenate([-sine, cosine], 1)], 0)
    return rows.astype(jnp.bfloat16)


def round_up(value, unit):
    return -(-value // unit) * unit


def swap_groups(arrays, width):
    arrays = list(arrays)
    lane = lax.broadcasted_iota(jnp.int32, (1, LANES), 1)
    bit = 1
    while bit < len(arrays):
        low = (lane // width) % (2 * bit) < bit
        for index in range(len(arrays)):
            if index & bit:
                continue
            first, second = arrays[index], arrays[index + bit]
            arrays[index] = jnp.where(low, first, pltpu.roll(second, bit * width, 1))
            arrays[index + bit] = jnp.where(low, pltpu.roll(first, LANES - bit * width, 1), second)
        bit *= 2
    return arrays


def invert(gram, ridge):
    pairs = len(gram)
    snaps = gram[0].shape[0] // 2
    lane = lax.broadcasted_iota(jnp.int32, (snaps, 2 * snaps), 1)
    line = lax.broadcasted_iota(jnp.int32, (snaps, 2 * snaps), 0)
    sign = jnp.where(lax.broadcasted_iota(jnp.int32, (1, 2 * snaps), 1) < snaps, -1.0, 1.0)
    grams = []
    states = []
    for pair in range(pairs):
        whole = gram[pair]
        swapped = pltpu.roll(whole[snaps:], snaps, 1)
        top = whole[:snaps] + jnp.where(lane < snaps, swapped, 0.0)
        top = jnp.where(lane < snaps, top, swapped - whole[:snaps])
        grams.append(top)
        states.append(top + jnp.where(line == lane, ridge[pair], 0.0))
    for k in range(0, snaps, 2):
        near, far = line == k, line == k + 1
        column = (lane // 2 == k // 2) | (lane // 2 == (snaps + k) // 2)
        unit = jnp.where((near | far) & (lane == line), 1.0, 0.0)
        for pair in range(pairs):
            state = states[pair]
            first_re, second_re, first_im, second_im = (
                jnp.broadcast_to(state[:, at:at + 1], state.shape) for at in (k, k + 1, snaps + k, snaps + k + 1))
            head, tail = first_re[k:k + 1], second_re[k + 1:k + 2]
            cross_re, cross_im = second_re[k:k + 1], second_im[k:k + 1]
            inverse = 1.0 / (head * tail - (cross_re * cross_re + cross_im * cross_im))
            cleared = jnp.where(column, unit, state)
            one, two = cleared[k:k + 1], cleared[k + 1:k + 2]
            one_twin, two_twin = pltpu.roll(one, snaps, 1) * sign, pltpu.roll(two, snaps, 1) * sign
            top = (tail * one - (cross_re * two + cross_im * two_twin)) * inverse
            top_twin = (tail * one_twin - (cross_re * two_twin - cross_im * two)) * inverse
            low = (head * two - (cross_re * one - cross_im * one_twin)) * inverse
            low_twin = (head * two_twin - (cross_re * one_twin + cross_im * one)) * inverse
            fresh = cleared - ((first_re * top + first_im * top_twin) + (second_re * low + second_im * low_twin))
            states[pair] = jnp.where(near, top, jnp.where(far, low, fresh))
    return [jnp.dot(grams[pair], jnp.concatenate([states[pair], pltpu.roll(states[pair], snaps, 1) * sign], axis=0),
                    precision=HIGHEST, preferred_element_type=jnp.float32) for pair in range(pairs)]


class Sizes:
    def __init__(self, shape, pair_total, snap_count, height_count):
        self.snap_local, self.components, self.height_local, self.modes, self.parts, self.points = shape
        self.snap_count, self.height_count = snap_count, height_count
        self.owners = snap_count * height_count
        self.pairs = pair_total
        self.pair_local = pair_total // self.owners
        self.near = self.components * self.height_local
        self.snaps = snap_count * self.snap_local
        self.groups = LANES // self.snap_local
        self.tiles = self.near // self.groups
        self.tiles_each = self.height_local // self.groups
        self.columns = 2 * self.pairs
        self.kinds = 2 * self.pair_local
        self.sent = self.tiles * self.kinds
        self.out_stride = round_up(self.sent, TILE)
        self.back = self.sent + 1
        self.back_stride = round_up(self.back, TILE)
        self.wide = self.modes * self.parts * self.points
        self.half_heights = height_count // 2
        self.half_owners = snap_count * self.half_heights
        self.sets = 2 * snap_count // self.groups


def embed(top):
    snaps = top.shape[0]
    sign = jnp.where(lax.broadcasted_iota(jnp.int32, (1, 2 * snaps), 1) < snaps, -1.0, 1.0)
    return jnp.concatenate([top, pltpu.roll(top, snaps, 1) * sign], axis=0)


def whole_kernel(z, wave_hbm, list_hbm, ridge_hbm, x_hbm, y_hbm, predicted_ref, misfit_ref,
                 wave, list_ref, ridge_ref, x_buf, y_buf, table, x_out, y_out, x_in, y_in, x_rows, y_rows, s_out, s_in,
                 b_out, b_in, note_out, note_in,
                 load_sem, x_send, x_recv, y_send, y_recv, s_send, s_recv, b_send, b_recv, note_send, note_recv, own_sem):
    snap, height = lax.axis_index("snap"), lax.axis_index("height")
    half, inner = height // z.half_heights, lax.rem(height, z.half_heights)
    own_slot = snap * z.height_count + inner * 2 + half
    twin_slot = snap * z.height_count + inner * 2 + (1 - half)
    barrier = pltpu.get_barrier_semaphore()

    def wrap(value, count):
        return lax.rem(value + count, count)

    def slot_of(snap_at, height_at):
        return snap_at * z.height_count + lax.rem(height_at, z.half_heights) * 2 + height_at // z.half_heights

    def away(step):
        return wrap(snap + lax.rem(step, z.snap_count), z.snap_count), wrap(height + step // z.snap_count, z.height_count)

    def beside(step, sign, side):
        return (wrap(snap + sign * lax.rem(step, z.snap_count), z.snap_count),
                side * z.half_heights + wrap(inner + sign * (step // z.snap_count), z.half_heights))

    def load(source, target, part, index):
        span = pl.ds(part * z.height_local, z.height_local)
        return pltpu.make_async_copy(source.at[:, span], target.at[:, span], load_sem.at[index])

    small = [pltpu.make_async_copy(source, target, load_sem.at[2 * z.components + index])
             for index, (source, target) in enumerate([(list_hbm, list_ref), (wave_hbm, wave), (ridge_hbm, ridge_ref)])]
    for item in small:
        item.start()
    x_loads = [load(x_hbm, x_buf, part, part) for part in range(z.components)]
    y_loads = [load(y_hbm, y_buf, part, z.components + part) for part in range(z.components)]
    for item in x_loads + y_loads:
        item.start()

    def greet(step, carry):
        pl.semaphore_signal(barrier, inc=1, device_id=away(step), device_id_type=pl.DeviceIdType.MESH)
        return carry

    lax.fori_loop(1, z.owners, greet, 0)

    same = (lax.broadcasted_iota(jnp.int32, (z.pairs, z.pairs), 0)
            == lax.broadcasted_iota(jnp.int32, (z.pairs, z.pairs), 1))
    small[0].wait()
    mode = jnp.sum(jnp.where(same, list_ref[0:1, :], 0), axis=1, keepdims=True)
    number = jnp.sum(jnp.where(same, list_ref[1:2, :], 0), axis=1, keepdims=True)
    mode = jnp.concatenate([mode, mode], axis=0)
    number = jnp.concatenate([number, number + z.points], axis=0)
    chosen = lax.broadcasted_iota(jnp.int32, (z.columns, 2 * z.points), 1) == number
    small[1].wait()
    picked = jnp.dot(jnp.where(chosen, 1.0, 0.0).astype(jnp.bfloat16), wave[...], preferred_element_type=jnp.float32)
    for index in range(z.modes):
        table[:, index * 2 * z.points:(index + 1) * 2 * z.points] = jnp.where(mode == index, picked, 0.0).astype(jnp.bfloat16)
    x_rows[...] = jnp.zeros_like(x_rows)
    y_rows[...] = jnp.zeros_like(y_rows)

    def spectrum(buf, loads, out):
        for part in range(z.components):
            loads[part].wait()
            rows = jnp.concatenate([buf[:, part * z.height_local + index].reshape(z.snap_local, z.wide)
                                    for index in range(z.height_local)], axis=0)
            product = lax.dot_general(table[...], rows, (((1,), (1,)), ((), ())), preferred_element_type=jnp.float32)
            for each in range(z.tiles_each):
                tile = part * z.tiles_each + each
                for kind in range(z.kinds):
                    out[pl.ds(tile * z.kinds + kind, z.owners, stride=z.out_stride), :] = (
                        product[kind * z.owners:(kind + 1) * z.owners, each * LANES:(each + 1) * LANES])

    def at(index, stride, rows):
        return pl.ds(pl.multiple_of(index * stride, TILE), rows)

    def remote(source, target, send, recv, where):
        return pltpu.make_async_remote_copy(src_ref=source, dst_ref=target, send_sem=send, recv_sem=recv, device_id=where,
                                            device_id_type=pl.DeviceIdType.MESH)

    def each(copy, first, last, act):
        def one(step, carry):
            act(copy(step))
            return carry
        lax.fori_loop(first, last, one, 0)

    def start(item):
        item.start()

    def sent(item):
        item.wait_send()

    def arrived(item):
        item.wait_recv()

    def x_copy(step):
        where = away(step)
        return remote(x_out.at[at(slot_of(*where), z.out_stride, z.sent)], x_in.at[at(step, z.out_stride, z.sent)],
                      x_send.at[step], x_recv.at[step], where)

    def y_copy(step):
        where = beside(step, 1, half)
        first = where[0] * z.height_count + lax.rem(where[1], z.half_heights) * 2
        return remote(y_out.at[at(first, z.out_stride, 2 * z.out_stride)], y_in.at[at(step, 2 * z.out_stride, 2 * z.out_stride)],
                      y_send.at[step], y_recv.at[step], where)

    def b_copy(side, target):
        def copy(step):
            return remote(b_out.at[side, at(step, z.back_stride, z.back)], b_in.at[at(target, z.back_stride, z.back)],
                          b_send.at[side, step], b_recv.at[side, step], beside(step, -1, half))
        return copy

    def note_copy(step):
        return remote(note_out.at[pl.ds(0, 1)], note_in.at[at(step, TILE, 1)], note_send.at[step], note_recv.at[step],
                      beside(step, 1, 1 - half))

    x_kept = pltpu.make_async_copy(x_out.at[at(own_slot, z.out_stride, z.sent)], x_in.at[at(0, z.out_stride, z.sent)], own_sem.at[0])
    y_kept = pltpu.make_async_copy(
        y_out.at[at(snap * z.height_count + inner * 2, z.out_stride, 2 * z.out_stride)],
        y_in.at[at(0, 2 * z.out_stride, 2 * z.out_stride)], own_sem.at[1])
    slots = (own_slot, twin_slot)
    b_kept = [pltpu.make_async_copy(b_out.at[side, at(0, z.back_stride, z.back)], b_in.at[at(slots[side], z.back_stride, z.back)],
                                    own_sem.at[2 + side]) for side in range(2)]
    s_copy = remote(s_out, s_in, s_send, s_recv, (snap, (1 - half) * z.half_heights + inner))

    spectrum(x_buf, x_loads, x_out)
    pl.semaphore_wait(barrier, z.owners - 1)
    x_kept.start()
    each(x_copy, 1, z.owners, start)
    spectrum(y_buf, y_loads, y_out)
    y_kept.start()
    each(y_copy, 1, z.half_owners, start)

    def place(base, index, pair):
        part, member = index // z.snap_count, index % z.snap_count
        return base(member) + part * z.pair_local + pair

    def gather(source, base, pair, target, block):
        for group in range(z.sets):
            moved = swap_groups([source[pl.ds(place(base, group * z.groups + index, pair), z.tiles, stride=z.kinds), :]
                                 for index in range(z.groups)], z.snap_local)
            for index, piece in enumerate(moved):
                target[pl.ds((block * z.groups + index) * TILE, z.tiles), group * LANES:(group + 1) * LANES] = piece

    gram = [None] * z.pair_local
    batch = min(4, z.height_count)
    span = batch * z.groups * TILE
    for block in range(z.height_count):
        for member in range(z.snap_count):
            step = block * z.snap_count + member
            if step == 0:
                x_kept.wait()
            else:
                x_copy(step).wait_recv()
        for pair in range(z.pair_local):
            gather(x_in, lambda member: (block * z.snap_count + member) * z.out_stride, pair, x_rows.at[pair], block)
            if block % batch == batch - 1:
                rows = x_rows[pair, pl.ds((block // batch) * span, span), :]
                term = lax.dot_general(rows, rows, (((0,), (0,)), ((), ())), precision=HIGHEST, preferred_element_type=jnp.float32)
                gram[pair] = term if gram[pair] is None else gram[pair] + term
    def collect(side):
        which = half if side == 0 else 1 - half
        for pair in range(z.pair_local):
            for block in range(z.half_heights):
                gather(y_in, lambda member: ((block * z.snap_count + member) * 2 + which) * z.out_stride, pair,
                       y_rows.at[side, pair], block)

    small[2].wait()
    ridge = []
    for pair in range(z.pair_local):
        mine = lax.broadcasted_iota(jnp.int32, (1, z.pairs), 1) == pair * z.owners + own_slot
        level = jnp.sum(jnp.where(mine, ridge_ref[...], 0), axis=1, keepdims=True)
        ridge.append(lax.shift_left(jnp.ones_like(level), level).astype(jnp.float32) * (0.25 * z.snaps))
    tops = invert(gram, ridge)
    for pair in range(z.pair_local):
        s_out[pair] = tops[pair]
    s_copy.start()

    lane = lax.broadcasted_iota(jnp.int32, (1, LANES), 1)

    def fit(side, tops):
        misses = jnp.zeros((1, 1), jnp.float32)
        energy = jnp.zeros((1, 1), jnp.float32)
        outcome = []
        for pair in range(z.pair_local):
            target = y_rows[side, pair]
            fitted = lax.dot_general(target, embed(tops[pair]), (((1,), (1,)), ((), ())), precision=HIGHEST,
                                     preferred_element_type=jnp.float32)
            gap = target - fitted
            misses = misses + jnp.sum(gap * gap, keepdims=True)
            energy = energy + jnp.sum(target * target, keepdims=True)
            outcome.append(fitted)
        return outcome, jnp.where(lane == 0, misses, jnp.where(lane == 1, energy, 0.0))

    def regroup(side, outcome, note):
        for pair in range(z.pair_local):
            for block in range(z.half_heights):
                for group in range(z.sets):
                    moved = swap_groups([outcome[pair][(block * z.groups + index) * TILE:(block * z.groups + index + 1) * TILE,
                                                       group * LANES:(group + 1) * LANES] for index in range(z.groups)], z.snap_local)
                    for index, piece in enumerate(moved):
                        row = place(lambda member: (block * z.snap_count + member) * z.back_stride, group * z.groups + index, pair)
                        b_out[side, pl.ds(row, z.tiles, stride=z.kinds), :] = piece[:z.tiles]
        b_out[side, pl.ds(z.sent, z.half_owners, stride=z.back_stride), :] = jnp.broadcast_to(note, (z.half_owners, LANES))

    y_kept.wait()
    each(y_copy, 1, z.half_owners, arrived)
    collect(0)
    outcome, note = fit(0, tops)
    regroup(0, outcome, note)
    b_kept[0].start()
    each(b_copy(0, own_slot), 1, z.half_owners, start)
    collect(1)
    s_copy.wait_recv()
    outcome, twin_note = fit(1, [s_in[pair] for pair in range(z.pair_local)])
    note_out[...] = jnp.broadcast_to(note + twin_note, note_out.shape)
    each(note_copy, 0, z.half_owners, start)
    regroup(1, outcome, twin_note)
    b_kept[1].start()
    each(b_copy(1, twin_slot), 1, z.half_owners, start)

    each(x_copy, 1, z.owners, sent)
    each(y_copy, 1, z.half_owners, sent)
    s_copy.wait_send()
    for side in range(2):
        b_kept[side].wait()
        each(b_copy(side, slots[side]), 1, z.half_owners, arrived)
    each(note_copy, 0, z.half_owners, arrived)

    for tile in range(z.tiles):
        for part in range(2):
            sheet = jnp.concatenate([b_in[pl.ds(tile * z.kinds + part * z.pair_local + pair, z.owners, stride=z.back_stride), :]
                                     for pair in range(z.pair_local)], axis=0)
            turned = sheet.T
            for index in range(z.groups):
                first = (tile * z.groups + index) * 2 + part
                piece = turned[index * z.snap_local:(index + 1) * z.snap_local]
                if z.pairs <= LANES:
                    predicted_ref[pl.ds(first, z.snap_local, stride=2 * z.near), :] = piece
                else:
                    for line in range(z.snap_local):
                        predicted_ref[pl.ds(first + line * 2 * z.near, 1), :] = piece[line:line + 1]
    notes = (jnp.sum(b_in[pl.ds(z.sent, z.owners, stride=z.back_stride), :], axis=0, keepdims=True)
             + jnp.sum(note_in[pl.ds(0, z.half_owners, stride=TILE), :], axis=0, keepdims=True))
    misfit_ref[...] = notes[:, 0:1] / notes[:, 1:2]
    for side in range(2):
        each(b_copy(side, slots[side]), 1, z.half_owners, sent)
    each(note_copy, 0, z.half_owners, sent)


def per_device(resolved, drain, pair_list, ridge_index):
    z = Sizes(resolved.shape, pair_list.shape[0], lax.axis_size("snap"), lax.axis_size("height"))
    vmem = pl.BlockSpec(memory_space=pltpu.VMEM)
    hbm = pl.BlockSpec(memory_space=pltpu.HBM)
    block = (z.snap_local, z.near, z.modes * z.parts, z.points)
    out_rows = z.owners * z.out_stride
    back_rows = z.half_owners * z.back_stride
    gathered = z.groups * TILE
    dma = pltpu.SemaphoreType.DMA
    stay = functools.partial(pltpu.with_memory_space_constraint, memory_space=pltpu.HBM)
    predicted, misfit = pl.pallas_call(
        functools.partial(whole_kernel, z),
        in_specs=[hbm] * 5,
        out_specs=[vmem, vmem],
        out_shape=[jax.ShapeDtypeStruct((z.snap_local * z.near * 2, z.pairs), jnp.float32),
                   jax.ShapeDtypeStruct((1, 1), jnp.float32)],
        scratch_shapes=[
            pltpu.VMEM((2 * z.points, 2 * z.points), jnp.bfloat16),
            pltpu.VMEM((2, z.pairs), jnp.int32),
            pltpu.VMEM((1, z.pairs), jnp.int32),
            pltpu.VMEM(block, jnp.bfloat16),
            pltpu.VMEM(block, jnp.bfloat16),
            pltpu.VMEM((z.columns, z.wide), jnp.bfloat16),
            pltpu.VMEM((out_rows, LANES), jnp.float32),
            pltpu.VMEM((out_rows, LANES), jnp.float32),
            pltpu.VMEM((out_rows, LANES), jnp.float32),
            pltpu.VMEM((out_rows, LANES), jnp.float32),
            pltpu.VMEM((z.pair_local, z.height_count * gathered, 2 * z.snaps), jnp.float32),
            pltpu.VMEM((2, z.pair_local, z.half_heights * gathered, 2 * z.snaps), jnp.float32),
            pltpu.VMEM((z.pair_local, z.snaps, 2 * z.snaps), jnp.float32),
            pltpu.VMEM((z.pair_local, z.snaps, 2 * z.snaps), jnp.float32),
            pltpu.VMEM((2, back_rows, LANES), jnp.float32),
            pltpu.VMEM((2 * back_rows, LANES), jnp.float32),
            pltpu.VMEM((TILE, LANES), jnp.float32),
            pltpu.VMEM((z.half_owners * TILE, LANES), jnp.float32),
            dma((2 * z.components + 3,)),
            dma((z.owners,)), dma((z.owners,)),
            dma((z.half_owners,)), dma((z.half_owners,)),
            dma, dma,
            dma((2, z.half_owners)), dma((2, z.half_owners)),
            dma((z.half_owners,)), dma((z.half_owners,)),
            dma((4,)),
        ],
        compiler_params=pltpu.CompilerParams(collective_id=0, has_side_effects=True, vmem_limit_bytes=VMEM_BYTES),
    )(stay(jnp.asarray(wave_table(z.points))), stay(pair_list.T), stay(ridge_index.reshape(1, z.pairs)),
      resolved.reshape(block), drain.reshape(block))
    predicted = predicted.reshape(z.snap_local, z.components, z.height_local, 2, z.pairs)
    return (predicted, misfit.reshape(1))


def solution(mesh):
    return jax.shard_map(
        per_device,
        mesh=mesh,
        in_specs=(
            P("snap", None, "height", None, None, None),
            P("snap", None, "height", None, None, None),
            P(),
            P(),
        ),
        out_specs=(P("snap", None, "height", None, None), P()),
        check_vma=False,
    )
```

```python
import functools
import math

import jax
import jax.numpy as jnp
import numpy as np
from jax import lax
from jax.experimental import pallas as pl
from jax.experimental.pallas import tpu as pltpu
from jax.sharding import PartitionSpec as P

HIGHEST = lax.Precision.HIGHEST
LANES = 128
TILE = 8
VMEM_BYTES = 48 << 20


def wave_table(points):
    grid = np.arange(points)
    theta = (grid[:, None] * grid[None, :] % points).astype(np.float32) * np.float32(2.0 * math.pi / points)
    scaling = np.float32(1.0 / math.sqrt(points))
    cosine = (np.cos(theta) * scaling).T
    sine = (np.sin(theta) * scaling).T
    rows = np.concatenate([np.concatenate([cosine, sine], 1), np.concatenate([-sine, cosine], 1)], 0)
    return rows.astype(jnp.bfloat16)


def round_up(value, unit):
    return -(-value // unit) * unit


def swap_groups(arrays, width):
    arrays = list(arrays)
    lane = lax.broadcasted_iota(jnp.int32, (1, LANES), 1)
    bit = 1
    while bit < len(arrays):
        low = (lane // width) % (2 * bit) < bit
        for index in range(len(arrays)):
            if index & bit:
                continue
            first, second = arrays[index], arrays[index + bit]
            arrays[index] = jnp.where(low, first, pltpu.roll(second, bit * width, 1))
            arrays[index + bit] = jnp.where(low, pltpu.roll(first, LANES - bit * width, 1), second)
        bit *= 2
    return arrays


def fold(whole):
    snaps = whole.shape[0] // 2
    lane = lax.broadcasted_iota(jnp.int32, (snaps, 2 * snaps), 1)
    swapped = pltpu.roll(whole[snaps:], snaps, 1)
    return jnp.where(lane < snaps, whole[:snaps] + swapped, swapped - whole[:snaps])


def invert(grams, ridge):
    pairs = len(grams)
    snaps = grams[0].shape[0]
    lane = lax.broadcasted_iota(jnp.int32, (snaps, 2 * snaps), 1)
    line = lax.broadcasted_iota(jnp.int32, (snaps, 2 * snaps), 0)
    sign = jnp.where(lax.broadcasted_iota(jnp.int32, (1, 2 * snaps), 1) < snaps, -1.0, 1.0)
    states = [grams[pair] + jnp.where(line == lane, ridge[pair], 0.0) for pair in range(pairs)]
    for k in range(0, snaps, 2):
        near, far = line == k, line == k + 1
        column = (lane // 2 == k // 2) | (lane // 2 == (snaps + k) // 2)
        unit = jnp.where((near | far) & (lane == line), 1.0, 0.0)
        for pair in range(pairs):
            state = states[pair]
            first_re, second_re, first_im, second_im = (
                jnp.broadcast_to(state[:, at:at + 1], state.shape) for at in (k, k + 1, snaps + k, snaps + k + 1))
            head, tail = first_re[k:k + 1], second_re[k + 1:k + 2]
            cross_re, cross_im = second_re[k:k + 1], second_im[k:k + 1]
            inverse = 1.0 / (head * tail - (cross_re * cross_re + cross_im * cross_im))
            cleared = jnp.where(column, unit, state)
            one, two = cleared[k:k + 1], cleared[k + 1:k + 2]
            one_twin, two_twin = pltpu.roll(one, snaps, 1) * sign, pltpu.roll(two, snaps, 1) * sign
            top = (tail * one - (cross_re * two + cross_im * two_twin)) * inverse
            top_twin = (tail * one_twin - (cross_re * two_twin - cross_im * two)) * inverse
            low = (head * two - (cross_re * one - cross_im * one_twin)) * inverse
            low_twin = (head * two_twin - (cross_re * one_twin + cross_im * one)) * inverse
            fresh = cleared - ((first_re * top + first_im * top_twin) + (second_re * low + second_im * low_twin))
            states[pair] = jnp.where(near, top, jnp.where(far, low, fresh))
    return [jnp.dot(grams[pair], jnp.concatenate([states[pair], pltpu.roll(states[pair], snaps, 1) * sign], axis=0),
                    precision=HIGHEST, preferred_element_type=jnp.float32) for pair in range(pairs)]


class Sizes:
    def __init__(self, shape, pair_total, snap_count, height_count):
        self.snap_local, self.components, self.height_local, self.modes, self.parts, self.points = shape
        self.snap_count, self.height_count = snap_count, height_count
        self.owners = snap_count * height_count
        self.pairs = pair_total
        self.pair_local = pair_total // self.owners
        self.near = self.components * self.height_local
        self.snaps = snap_count * self.snap_local
        self.groups = LANES // self.snap_local
        self.tiles = self.near // self.groups
        self.tiles_each = self.height_local // self.groups
        self.columns = 2 * self.pairs
        self.kinds = 2 * self.pair_local
        self.sent = self.tiles * self.kinds
        self.out_stride = round_up(self.sent, TILE)
        self.back = self.sent + 1
        self.back_stride = round_up(self.back, TILE)
        self.wide = self.modes * self.parts * self.points
        self.half_heights = height_count // 2
        self.half_owners = snap_count * self.half_heights
        self.sets = 2 * snap_count // self.groups


def embed(top):
    snaps = top.shape[0]
    sign = jnp.where(lax.broadcasted_iota(jnp.int32, (1, 2 * snaps), 1) < snaps, -1.0, 1.0)
    return jnp.concatenate([top, pltpu.roll(top, snaps, 1) * sign], axis=0)


def pack(tops):
    snaps = tops[0].shape[0]
    lane = lax.broadcasted_iota(jnp.int32, (snaps, 2 * snaps), 1)
    line = lax.broadcasted_iota(jnp.int32, (snaps, 2 * snaps), 0)
    first = jnp.where(line >= lane, tops[0], pltpu.roll(tops[0], snaps, 1))
    second = jnp.where(line >= lane - snaps, pltpu.roll(tops[1], snaps, 1), tops[1])
    return jnp.where(lane < snaps, first, second)


def unpack(packed):
    snaps = packed.shape[0]
    lane = lax.broadcasted_iota(jnp.int32, (snaps, snaps), 1)
    line = lax.broadcasted_iota(jnp.int32, (snaps, snaps), 0)
    turned = packed.T
    tops = []
    for pair in range(2):
        plain, other = packed[:, pair * snaps:(pair + 1) * snaps], turned[pair * snaps:(pair + 1) * snaps]
        real = jnp.where(line >= lane, plain, other)
        imaginary = jnp.where(line < lane, plain, jnp.where(line > lane, -other, 0.0))
        tops.append(jnp.concatenate([real, imaginary], axis=1))
    return tops


def whole_kernel(z, wave_hbm, list_hbm, ridge_hbm, x_hbm, y_hbm, predicted_ref, misfit_ref,
                 wave, list_ref, ridge_ref, x_buf, y_buf, table, x_out, y_out, x_in, y_in, x_rows, y_rows, g_out, g_in, s_out, s_in,
                 b_out, b_in, note_out, note_in,
                 load_sem, x_send, x_recv, y_send, y_recv, g_send, g_recv, s_send, s_recv, b_send, b_recv, note_send, note_recv, own_sem):
    snap, height = lax.axis_index("snap"), lax.axis_index("height")
    half, inner = height // z.half_heights, lax.rem(height, z.half_heights)
    own_slot = snap * z.height_count + inner * 2 + half
    twin_slot = snap * z.height_count + inner * 2 + (1 - half)
    barrier = pltpu.get_barrier_semaphore()

    def wrap(value, count):
        return lax.rem(value + count, count)

    def away(step):
        return wrap(snap + lax.rem(step, z.snap_count), z.snap_count), wrap(height + step // z.snap_count, z.height_count)

    def beside(step, sign, side):
        return (wrap(snap + sign * lax.rem(step, z.snap_count), z.snap_count),
                side * z.half_heights + wrap(inner + sign * (step // z.snap_count), z.half_heights))

    def load(source, target, part, index):
        span = pl.ds(part * z.height_local, z.height_local)
        return pltpu.make_async_copy(source.at[:, span], target.at[:, span], load_sem.at[index])

    small = [pltpu.make_async_copy(source, target, load_sem.at[2 * z.components + index])
             for index, (source, target) in enumerate([(list_hbm, list_ref), (wave_hbm, wave), (ridge_hbm, ridge_ref)])]
    for item in small:
        item.start()
    x_loads = [load(x_hbm, x_buf, part, part) for part in range(z.components)]
    y_loads = [load(y_hbm, y_buf, part, z.components + part) for part in range(z.components)]
    for item in x_loads + y_loads:
        item.start()

    def greet(step, carry):
        pl.semaphore_signal(barrier, inc=1, device_id=away(step), device_id_type=pl.DeviceIdType.MESH)
        return carry

    lax.fori_loop(1, z.owners, greet, 0)

    same = (lax.broadcasted_iota(jnp.int32, (z.pairs, z.pairs), 0)
            == lax.broadcasted_iota(jnp.int32, (z.pairs, z.pairs), 1))
    small[0].wait()
    mode = jnp.sum(jnp.where(same, list_ref[0:1, :], 0), axis=1, keepdims=True)
    number = jnp.sum(jnp.where(same, list_ref[1:2, :], 0), axis=1, keepdims=True)
    mode = jnp.concatenate([mode, mode], axis=0)
    number = jnp.concatenate([number, number + z.points], axis=0)
    chosen = lax.broadcasted_iota(jnp.int32, (z.columns, 2 * z.points), 1) == number
    small[1].wait()
    picked = jnp.dot(jnp.where(chosen, 1.0, 0.0).astype(jnp.bfloat16), wave[...], preferred_element_type=jnp.float32)
    for index in range(z.modes):
        table[:, index * 2 * z.points:(index + 1) * 2 * z.points] = jnp.where(mode == index, picked, 0.0).astype(jnp.bfloat16)
    x_rows[...] = jnp.zeros_like(x_rows)
    y_rows[...] = jnp.zeros_like(y_rows)

    def spectrum(buf, loads, out):
        for part in range(z.components):
            loads[part].wait()
            rows = jnp.concatenate([buf[:, part * z.height_local + index].reshape(z.snap_local, z.wide)
                                    for index in range(z.height_local)], axis=0)
            product = lax.dot_general(table[...], rows, (((1,), (1,)), ((), ())), preferred_element_type=jnp.float32)
            for each in range(z.tiles_each):
                tile = part * z.tiles_each + each
                for kind in range(z.kinds):
                    out[pl.ds(tile * z.kinds + kind, z.owners, stride=z.out_stride), :] = (
                        product[kind * z.owners:(kind + 1) * z.owners, each * LANES:(each + 1) * LANES])

    def at(index, stride, rows):
        return pl.ds(pl.multiple_of(index * stride, TILE), rows)

    def remote(source, target, send, recv, where):
        return pltpu.make_async_remote_copy(src_ref=source, dst_ref=target, send_sem=send, recv_sem=recv, device_id=where,
                                            device_id_type=pl.DeviceIdType.MESH)

    def each(copy, first, last, act):
        def one(step, carry):
            act(copy(step))
            return carry
        lax.fori_loop(first, last, one, 0)

    def start(item):
        item.start()

    def sent(item):
        item.wait_send()

    def arrived(item):
        item.wait_recv()

    def x_copy(side):
        def copy(step):
            where = beside(step, 1, half)
            slot = where[0] * z.height_count + lax.rem(where[1], z.half_heights) * 2 + (half if side == 0 else 1 - half)
            return remote(x_out.at[at(slot, z.out_stride, z.sent)], x_in.at[side, at(step, z.out_stride, z.sent)],
                          x_send.at[side, step], x_recv.at[side, step], where)
        return copy

    def y_copy(step):
        where = beside(step, 1, half)
        first = where[0] * z.height_count + lax.rem(where[1], z.half_heights) * 2
        return remote(y_out.at[at(first, z.out_stride, 2 * z.out_stride)], y_in.at[at(step, 2 * z.out_stride, 2 * z.out_stride)],
                      y_send.at[step], y_recv.at[step], where)

    def b_copy(side, target):
        def copy(step):
            return remote(b_out.at[side, at(step, z.back_stride, z.back)], b_in.at[at(target, z.back_stride, z.back)],
                          b_send.at[side, step], b_recv.at[side, step], beside(step, -1, half))
        return copy

    def note_copy(step):
        return remote(note_out.at[pl.ds(0, 1)], note_in.at[at(step, TILE, 1)], note_send.at[step], note_recv.at[step],
                      beside(step, 1, 1 - half))

    y_kept = pltpu.make_async_copy(
        y_out.at[at(snap * z.height_count + inner * 2, z.out_stride, 2 * z.out_stride)],
        y_in.at[at(0, 2 * z.out_stride, 2 * z.out_stride)], own_sem.at[1])
    slots = (own_slot, twin_slot)
    x_kept = [pltpu.make_async_copy(x_out.at[at(slots[side], z.out_stride, z.sent)], x_in.at[side, at(0, z.out_stride, z.sent)],
                                    own_sem.at[4 * side]) for side in range(2)]
    mirror = (snap, (1 - half) * z.half_heights + inner)
    g_copy = remote(g_out, g_in, g_send, g_recv, mirror)
    b_kept = [pltpu.make_async_copy(b_out.at[side, at(0, z.back_stride, z.back)], b_in.at[at(slots[side], z.back_stride, z.back)],
                                    own_sem.at[2 + side]) for side in range(2)]
    s_copy = remote(s_out, s_in, s_send, s_recv, mirror)

    spectrum(x_buf, x_loads, x_out)
    pl.semaphore_wait(barrier, z.owners - 1)
    for side in (1, 0):
        x_kept[side].start()
        each(x_copy(side), 1, z.half_owners, start)
    spectrum(y_buf, y_loads, y_out)

    def place(base, index, pair):
        part, member = index // z.snap_count, index % z.snap_count
        return base(member) + part * z.pair_local + pair

    def gather(source, base, pair, target, block):
        for group in range(z.sets):
            moved = swap_groups([source[pl.ds(place(base, group * z.groups + index, pair), z.tiles, stride=z.kinds), :]
                                 for index in range(z.groups)], z.snap_local)
            for index, piece in enumerate(moved):
                target[pl.ds((block * z.groups + index) * TILE, z.tiles), group * LANES:(group + 1) * LANES] = piece

    batch = min(4, z.half_heights)
    span = batch * z.groups * TILE

    def grams(side):
        found = [None] * z.pair_local
        for block in range(z.half_heights):
            for member in range(z.snap_count):
                step = block * z.snap_count + member
                if step == 0:
                    x_kept[side].wait()
                else:
                    x_copy(side)(step).wait_recv()
            for pair in range(z.pair_local):
                gather(x_in.at[side], lambda member: (block * z.snap_count + member) * z.out_stride, pair, x_rows.at[side, pair], block)
                if block % batch == batch - 1:
                    rows = x_rows[side, pair, pl.ds((block // batch) * span, span), :]
                    term = lax.dot_general(rows, rows, (((0,), (0,)), ((), ())), precision=HIGHEST,
                                           preferred_element_type=jnp.float32)
                    found[pair] = term if found[pair] is None else found[pair] + term
        return [pack([fold(found[index]), fold(found[index + 1])]) for index in range(0, z.pair_local, 2)]

    for index, packed in enumerate(grams(1)):
        g_out[index] = packed
    g_copy.start()
    y_kept.start()
    each(y_copy, 1, z.half_owners, start)
    own_grams = grams(0)
    g_copy.wait_recv()
    tops = [top for index, packed in enumerate(own_grams) for top in unpack(packed + g_in[index])]
    def collect(side):
        which = half if side == 0 else 1 - half
        for pair in range(z.pair_local):
            for block in range(z.half_heights):
                gather(y_in, lambda member: ((block * z.snap_count + member) * 2 + which) * z.out_stride, pair,
                       y_rows.at[side, pair], block)

    small[2].wait()
    ridge = []
    for pair in range(z.pair_local):
        mine = lax.broadcasted_iota(jnp.int32, (1, z.pairs), 1) == pair * z.owners + own_slot
        level = jnp.sum(jnp.where(mine, ridge_ref[...], 0), axis=1, keepdims=True)
        ridge.append(lax.shift_left(jnp.ones_like(level), level).astype(jnp.float32) * (0.25 * z.snaps))
    tops = invert(tops, ridge)
    for index in range(z.pair_local // 2):
        s_out[index] = pack(tops[2 * index:2 * index + 2])
    s_copy.start()

    lane = lax.broadcasted_iota(jnp.int32, (1, LANES), 1)

    def fit(side, tops):
        misses = jnp.zeros((1, 1), jnp.float32)
        energy = jnp.zeros((1, 1), jnp.float32)
        outcome = []
        for pair in range(z.pair_local):
            target = y_rows[side, pair]
            fitted = lax.dot_general(target, embed(tops[pair]), (((1,), (1,)), ((), ())), precision=HIGHEST,
                                     preferred_element_type=jnp.float32)
            gap = target - fitted
            misses = misses + jnp.sum(gap * gap, keepdims=True)
            energy = energy + jnp.sum(target * target, keepdims=True)
            outcome.append(fitted)
        return outcome, jnp.where(lane == 0, misses, jnp.where(lane == 1, energy, 0.0))

    def regroup(side, outcome, note):
        for pair in range(z.pair_local):
            for block in range(z.half_heights):
                for group in range(z.sets):
                    moved = swap_groups([outcome[pair][(block * z.groups + index) * TILE:(block * z.groups + index + 1) * TILE,
                                                       group * LANES:(group + 1) * LANES] for index in range(z.groups)], z.snap_local)
                    for index, piece in enumerate(moved):
                        row = place(lambda member: (block * z.snap_count + member) * z.back_stride, group * z.groups + index, pair)
                        b_out[side, pl.ds(row, z.tiles, stride=z.kinds), :] = piece[:z.tiles]
        b_out[side, pl.ds(z.sent, z.half_owners, stride=z.back_stride), :] = jnp.broadcast_to(note, (z.half_owners, LANES))

    y_kept.wait()
    each(y_copy, 1, z.half_owners, arrived)
    collect(0)
    outcome, note = fit(0, tops)
    regroup(0, outcome, note)
    b_kept[0].start()
    each(b_copy(0, own_slot), 1, z.half_owners, start)
    collect(1)
    s_copy.wait_recv()
    outcome, twin_note = fit(1, [top for index in range(z.pair_local // 2) for top in unpack(s_in[index])])
    note_out[...] = jnp.broadcast_to(note + twin_note, note_out.shape)
    each(note_copy, 0, z.half_owners, start)
    regroup(1, outcome, twin_note)
    b_kept[1].start()
    each(b_copy(1, twin_slot), 1, z.half_owners, start)

    for side in range(2):
        each(x_copy(side), 1, z.half_owners, sent)
    g_copy.wait_send()
    each(y_copy, 1, z.half_owners, sent)
    s_copy.wait_send()
    for side in range(2):
        b_kept[side].wait()
        each(b_copy(side, slots[side]), 1, z.half_owners, arrived)
    each(note_copy, 0, z.half_owners, arrived)

    for tile in range(z.tiles):
        for part in range(2):
            sheet = jnp.concatenate([b_in[pl.ds(tile * z.kinds + part * z.pair_local + pair, z.owners, stride=z.back_stride), :]
                                     for pair in range(z.pair_local)], axis=0)
            turned = sheet.T
            for index in range(z.groups):
                first = (tile * z.groups + index) * 2 + part
                piece = turned[index * z.snap_local:(index + 1) * z.snap_local]
                if z.pairs <= LANES:
                    predicted_ref[pl.ds(first, z.snap_local, stride=2 * z.near), :] = piece
                else:
                    for line in range(z.snap_local):
                        predicted_ref[pl.ds(first + line * 2 * z.near, 1), :] = piece[line:line + 1]
    notes = (jnp.sum(b_in[pl.ds(z.sent, z.owners, stride=z.back_stride), :], axis=0, keepdims=True)
             + jnp.sum(note_in[pl.ds(0, z.half_owners, stride=TILE), :], axis=0, keepdims=True))
    misfit_ref[...] = notes[:, 0:1] / notes[:, 1:2]
    for side in range(2):
        each(b_copy(side, slots[side]), 1, z.half_owners, sent)
    each(note_copy, 0, z.half_owners, sent)


def per_device(resolved, drain, pair_list, ridge_index):
    z = Sizes(resolved.shape, pair_list.shape[0], lax.axis_size("snap"), lax.axis_size("height"))
    vmem = pl.BlockSpec(memory_space=pltpu.VMEM)
    hbm = pl.BlockSpec(memory_space=pltpu.HBM)
    block = (z.snap_local, z.near, z.modes * z.parts, z.points)
    out_rows = z.owners * z.out_stride
    back_rows = z.half_owners * z.back_stride
    gathered = z.groups * TILE
    dma = pltpu.SemaphoreType.DMA
    stay = functools.partial(pltpu.with_memory_space_constraint, memory_space=pltpu.HBM)
    predicted, misfit = pl.pallas_call(
        functools.partial(whole_kernel, z),
        in_specs=[hbm] * 5,
        out_specs=[vmem, vmem],
        out_shape=[jax.ShapeDtypeStruct((z.snap_local * z.near * 2, z.pairs), jnp.float32),
                   jax.ShapeDtypeStruct((1, 1), jnp.float32)],
        scratch_shapes=[
            pltpu.VMEM((2 * z.points, 2 * z.points), jnp.bfloat16),
            pltpu.VMEM((2, z.pairs), jnp.int32),
            pltpu.VMEM((1, z.pairs), jnp.int32),
            pltpu.VMEM(block, jnp.bfloat16),
            pltpu.VMEM(block, jnp.bfloat16),
            pltpu.VMEM((z.columns, z.wide), jnp.bfloat16),
            pltpu.VMEM((out_rows, LANES), jnp.float32),
            pltpu.VMEM((out_rows, LANES), jnp.float32),
            pltpu.VMEM((2, z.half_owners * z.out_stride, LANES), jnp.float32),
            pltpu.VMEM((out_rows, LANES), jnp.float32),
            pltpu.VMEM((2, z.pair_local, z.half_heights * gathered, 2 * z.snaps), jnp.float32),
            pltpu.VMEM((2, z.pair_local, z.half_heights * gathered, 2 * z.snaps), jnp.float32),
            pltpu.VMEM((z.pair_local // 2, z.snaps, 2 * z.snaps), jnp.float32),
            pltpu.VMEM((z.pair_local // 2, z.snaps, 2 * z.snaps), jnp.float32),
            pltpu.VMEM((z.pair_local // 2, z.snaps, 2 * z.snaps), jnp.float32),
            pltpu.VMEM((z.pair_local // 2, z.snaps, 2 * z.snaps), jnp.float32),
            pltpu.VMEM((2, back_rows, LANES), jnp.float32),
            pltpu.VMEM((2 * back_rows, LANES), jnp.float32),
            pltpu.VMEM((TILE, LANES), jnp.float32),
            pltpu.VMEM((z.half_owners * TILE, LANES), jnp.float32),
            dma((2 * z.components + 3,)),
            dma((2, z.half_owners)), dma((2, z.half_owners)),
            dma((z.half_owners,)), dma((z.half_owners,)),
            dma, dma,
            dma, dma,
            dma((2, z.half_owners)), dma((2, z.half_owners)),
            dma((z.half_owners,)), dma((z.half_owners,)),
            dma((5,)),
        ],
        compiler_params=pltpu.CompilerParams(collective_id=0, has_side_effects=True, vmem_limit_bytes=VMEM_BYTES),
    )(stay(jnp.asarray(wave_table(z.points))), stay(pair_list.T), stay(ridge_index.reshape(1, z.pairs)),
      resolved.reshape(block), drain.reshape(block))
    predicted = predicted.reshape(z.snap_local, z.components, z.height_local, 2, z.pairs)
    return (predicted, misfit.reshape(1))


def solution(mesh):
    return jax.shard_map(
        per_device,
        mesh=mesh,
        in_specs=(
            P("snap", None, "height", None, None, None),
            P("snap", None, "height", None, None, None),
            P(),
            P(),
        ),
        out_specs=(P("snap", None, "height", None, None), P()),
        check_vma=False,
    )
```

```python
import functools
import math

import jax
import jax.numpy as jnp
import numpy as np
from jax import lax
from jax.experimental import pallas as pl
from jax.experimental.pallas import tpu as pltpu
from jax.sharding import PartitionSpec as P

HIGHEST = lax.Precision.HIGHEST
LANES = 128
TILE = 8
VMEM_BYTES = 48 << 20
UNROLLED = 16


def wave_table(points):
    grid = np.arange(points)
    theta = (grid[:, None] * grid[None, :] % points).astype(np.float32) * np.float32(2.0 * math.pi / points)
    scaling = np.float32(1.0 / math.sqrt(points))
    cosine = (np.cos(theta) * scaling).T
    sine = (np.sin(theta) * scaling).T
    rows = np.concatenate([np.concatenate([cosine, sine], 1), np.concatenate([-sine, cosine], 1)], 0)
    return rows.astype(jnp.bfloat16)


def round_up(value, unit):
    return -(-value // unit) * unit


def swap_groups(arrays, width):
    arrays = list(arrays)
    lane = lax.broadcasted_iota(jnp.int32, (1, LANES), 1)
    bit = 1
    while bit < len(arrays):
        low = (lane // width) % (2 * bit) < bit
        for index in range(len(arrays)):
            if index & bit:
                continue
            first, second = arrays[index], arrays[index + bit]
            arrays[index] = jnp.where(low, first, pltpu.roll(second, bit * width, 1))
            arrays[index + bit] = jnp.where(low, pltpu.roll(first, LANES - bit * width, 1), second)
        bit *= 2
    return arrays


def fold(whole):
    snaps = whole.shape[0] // 2
    lane = lax.broadcasted_iota(jnp.int32, (snaps, 2 * snaps), 1)
    swapped = pltpu.roll(whole[snaps:], snaps, 1)
    return jnp.where(lane < snaps, whole[:snaps] + swapped, swapped - whole[:snaps])


def invert(grams, ridge):
    pairs = len(grams)
    snaps = grams[0].shape[0]
    lane = lax.broadcasted_iota(jnp.int32, (snaps, 2 * snaps), 1)
    line = lax.broadcasted_iota(jnp.int32, (snaps, 2 * snaps), 0)
    sign = jnp.where(lax.broadcasted_iota(jnp.int32, (1, 2 * snaps), 1) < snaps, -1.0, 1.0)
    states = [grams[pair] + jnp.where(line == lane, ridge[pair], 0.0) for pair in range(pairs)]
    for k in range(0, snaps, 2):
        near, far = line == k, line == k + 1
        column = (lane // 2 == k // 2) | (lane // 2 == (snaps + k) // 2)
        unit = jnp.where((near | far) & (lane == line), 1.0, 0.0)
        for pair in range(pairs):
            state = states[pair]
            first_re, second_re, first_im, second_im = (
                jnp.broadcast_to(state[:, at:at + 1], state.shape) for at in (k, k + 1, snaps + k, snaps + k + 1))
            head, tail = first_re[k:k + 1], second_re[k + 1:k + 2]
            cross_re, cross_im = second_re[k:k + 1], second_im[k:k + 1]
            inverse = 1.0 / (head * tail - (cross_re * cross_re + cross_im * cross_im))
            cleared = jnp.where(column, unit, state)
            one, two = cleared[k:k + 1], cleared[k + 1:k + 2]
            one_twin, two_twin = pltpu.roll(one, snaps, 1) * sign, pltpu.roll(two, snaps, 1) * sign
            top = (tail * one - (cross_re * two + cross_im * two_twin)) * inverse
            top_twin = (tail * one_twin - (cross_re * two_twin - cross_im * two)) * inverse
            low = (head * two - (cross_re * one - cross_im * one_twin)) * inverse
            low_twin = (head * two_twin - (cross_re * one_twin + cross_im * one)) * inverse
            fresh = cleared - ((first_re * top + first_im * top_twin) + (second_re * low + second_im * low_twin))
            states[pair] = jnp.where(near, top, jnp.where(far, low, fresh))
    return [jnp.dot(grams[pair], jnp.concatenate([states[pair], pltpu.roll(states[pair], snaps, 1) * sign], axis=0),
                    precision=HIGHEST, preferred_element_type=jnp.float32) for pair in range(pairs)]


class Sizes:
    def __init__(self, shape, pair_total, snap_count, height_count):
        self.snap_local, self.components, self.height_local, self.modes, self.parts, self.points = shape
        self.snap_count, self.height_count = snap_count, height_count
        self.owners = snap_count * height_count
        self.pairs = pair_total
        self.pair_local = pair_total // self.owners
        self.near = self.components * self.height_local
        self.snaps = snap_count * self.snap_local
        self.groups = LANES // self.snap_local
        self.tiles = self.near // self.groups
        self.tiles_each = self.height_local // self.groups
        self.columns = 2 * self.pairs
        self.kinds = 2 * self.pair_local
        self.sent = self.tiles * self.kinds
        self.out_stride = round_up(self.sent, TILE)
        self.back = self.sent + 1
        self.back_stride = round_up(self.back, TILE)
        self.wide = self.modes * self.parts * self.points
        self.half_heights = height_count // 2
        self.half_owners = snap_count * self.half_heights
        self.sets = 2 * snap_count // self.groups


def three(left, right):
    left_high, right_high = left.astype(jnp.bfloat16), right.astype(jnp.bfloat16)
    left_low = (left - left_high.astype(jnp.float32)).astype(jnp.bfloat16)
    right_low = (right - right_high.astype(jnp.float32)).astype(jnp.bfloat16)
    return lax.dot_general(jnp.concatenate([left_high, left_high, left_low], axis=1),
                           jnp.concatenate([right_high, right_low, right_high], axis=1),
                           (((1,), (1,)), ((), ())), preferred_element_type=jnp.float32)


def embed(top):
    snaps = top.shape[0]
    sign = jnp.where(lax.broadcasted_iota(jnp.int32, (1, 2 * snaps), 1) < snaps, -1.0, 1.0)
    return jnp.concatenate([top, pltpu.roll(top, snaps, 1) * sign], axis=0)


def pack(tops):
    snaps = tops[0].shape[0]
    lane = lax.broadcasted_iota(jnp.int32, (snaps, 2 * snaps), 1)
    line = lax.broadcasted_iota(jnp.int32, (snaps, 2 * snaps), 0)
    first = jnp.where(line >= lane, tops[0], pltpu.roll(tops[0], snaps, 1))
    second = jnp.where(line >= lane - snaps, pltpu.roll(tops[1], snaps, 1), tops[1])
    return jnp.where(lane < snaps, first, second)


def unpack(packed):
    snaps = packed.shape[0]
    lane = lax.broadcasted_iota(jnp.int32, (snaps, snaps), 1)
    line = lax.broadcasted_iota(jnp.int32, (snaps, snaps), 0)
    turned = packed.T
    tops = []
    for pair in range(2):
        plain, other = packed[:, pair * snaps:(pair + 1) * snaps], turned[pair * snaps:(pair + 1) * snaps]
        real = jnp.where(line >= lane, plain, other)
        imaginary = jnp.where(line < lane, plain, jnp.where(line > lane, -other, 0.0))
        tops.append(jnp.concatenate([real, imaginary], axis=1))
    return tops


def whole_kernel(z, wave_hbm, list_hbm, ridge_hbm, x_hbm, y_hbm, predicted_ref, misfit_ref,
                 wave, list_ref, ridge_ref, x_buf, y_buf, table, x_out, y_out, x_in, y_in, x_rows, y_rows, g_out, g_in, s_out, s_in,
                 b_out, b_in, note_out, note_in,
                 load_sem, x_send, x_recv, y_send, y_recv, g_send, g_recv, s_send, s_recv, b_send, b_recv, note_send, note_recv, own_sem):
    snap, height = lax.axis_index("snap"), lax.axis_index("height")
    half, inner = height // z.half_heights, lax.rem(height, z.half_heights)
    own_slot = snap * z.height_count + inner * 2 + half
    twin_slot = snap * z.height_count + inner * 2 + (1 - half)
    barrier = pltpu.get_barrier_semaphore()

    def wrap(value, count):
        return lax.rem(value + count, count)

    def away(step):
        return wrap(snap + lax.rem(step, z.snap_count), z.snap_count), wrap(height + step // z.snap_count, z.height_count)

    def beside(step, sign, side):
        return (wrap(snap + sign * lax.rem(step, z.snap_count), z.snap_count),
                side * z.half_heights + wrap(inner + sign * (step // z.snap_count), z.half_heights))

    def load(source, target, part, index):
        span = pl.ds(part * z.height_local, z.height_local)
        return pltpu.make_async_copy(source.at[:, span], target.at[:, span], load_sem.at[index])

    small = [pltpu.make_async_copy(source, target, load_sem.at[2 * z.components + index])
             for index, (source, target) in enumerate([(list_hbm, list_ref), (wave_hbm, wave), (ridge_hbm, ridge_ref)])]
    for item in small:
        item.start()
    x_loads = [load(x_hbm, x_buf, part, part) for part in range(z.components)]
    y_loads = [load(y_hbm, y_buf, part, z.components + part) for part in range(z.components)]
    for item in x_loads + y_loads:
        item.start()

    def greet(step, carry):
        pl.semaphore_signal(barrier, inc=1, device_id=away(step), device_id_type=pl.DeviceIdType.MESH)
        return carry

    lax.fori_loop(1, z.owners, greet, 0)

    same = (lax.broadcasted_iota(jnp.int32, (z.pairs, z.pairs), 0)
            == lax.broadcasted_iota(jnp.int32, (z.pairs, z.pairs), 1))
    small[0].wait()
    mode = jnp.sum(jnp.where(same, list_ref[0:1, :], 0), axis=1, keepdims=True)
    number = jnp.sum(jnp.where(same, list_ref[1:2, :], 0), axis=1, keepdims=True)
    mode = jnp.concatenate([mode, mode], axis=0)
    number = jnp.concatenate([number, number + z.points], axis=0)
    chosen = lax.broadcasted_iota(jnp.int32, (z.columns, 2 * z.points), 1) == number
    small[1].wait()
    picked = jnp.dot(jnp.where(chosen, 1.0, 0.0).astype(jnp.bfloat16), wave[...], preferred_element_type=jnp.float32)
    for index in range(z.modes):
        table[:, index * 2 * z.points:(index + 1) * 2 * z.points] = jnp.where(mode == index, picked, 0.0).astype(jnp.bfloat16)
    x_rows[...] = jnp.zeros_like(x_rows)
    y_rows[...] = jnp.zeros_like(y_rows)

    def spectrum(buf, loads, out):
        for part in range(z.components):
            loads[part].wait()
            rows = jnp.concatenate([buf[:, part * z.height_local + index].reshape(z.snap_local, z.wide)
                                    for index in range(z.height_local)], axis=0)
            product = lax.dot_general(table[...], rows, (((1,), (1,)), ((), ())), preferred_element_type=jnp.float32)
            for each in range(z.tiles_each):
                tile = part * z.tiles_each + each
                for kind in range(z.kinds):
                    out[pl.ds(tile * z.kinds + kind, z.owners, stride=z.out_stride), :] = (
                        product[kind * z.owners:(kind + 1) * z.owners, each * LANES:(each + 1) * LANES])

    def at(index, stride, rows):
        return pl.ds(pl.multiple_of(index * stride, TILE), rows)

    def remote(source, target, send, recv, where):
        return pltpu.make_async_remote_copy(src_ref=source, dst_ref=target, send_sem=send, recv_sem=recv, device_id=where,
                                            device_id_type=pl.DeviceIdType.MESH)

    def each(copy, first, last, act):
        def one(step, carry):
            act(copy(step))
            return carry
        if last > UNROLLED:
            lax.fori_loop(first, last, one, 0)
        else:
            for step in range(first, last):
                act(copy(step))

    def start(item):
        item.start()

    def sent(item):
        item.wait_send()

    def arrived(item):
        item.wait_recv()

    def x_copy(side):
        def copy(step):
            where = beside(step, 1, half)
            slot = where[0] * z.height_count + lax.rem(where[1], z.half_heights) * 2 + (half if side == 0 else 1 - half)
            return remote(x_out.at[at(slot, z.out_stride, z.sent)], x_in.at[side, at(step, z.out_stride, z.sent)],
                          x_send.at[side, step], x_recv.at[side, step], where)
        return copy

    def y_copy(step):
        where = beside(step, 1, half)
        first = where[0] * z.height_count + lax.rem(where[1], z.half_heights) * 2
        return remote(y_out.at[at(first, z.out_stride, 2 * z.out_stride)], y_in.at[at(step, 2 * z.out_stride, 2 * z.out_stride)],
                      y_send.at[step], y_recv.at[step], where)

    def b_copy(side, target):
        def copy(step):
            return remote(b_out.at[side, at(step, z.back_stride, z.back)], b_in.at[at(target, z.back_stride, z.back)],
                          b_send.at[side, step], b_recv.at[side, step], beside(step, -1, half))
        return copy

    def note_copy(step):
        return remote(note_out.at[pl.ds(0, 1)], note_in.at[at(step, TILE, 1)], note_send.at[step], note_recv.at[step],
                      beside(step, 1, 1 - half))

    y_kept = pltpu.make_async_copy(
        y_out.at[at(snap * z.height_count + inner * 2, z.out_stride, 2 * z.out_stride)],
        y_in.at[at(0, 2 * z.out_stride, 2 * z.out_stride)], own_sem.at[1])
    slots = (own_slot, twin_slot)
    x_kept = [pltpu.make_async_copy(x_out.at[at(slots[side], z.out_stride, z.sent)], x_in.at[side, at(0, z.out_stride, z.sent)],
                                    own_sem.at[4 * side]) for side in range(2)]
    mirror = (snap, (1 - half) * z.half_heights + inner)
    g_copy = remote(g_out, g_in, g_send, g_recv, mirror)
    b_kept = [pltpu.make_async_copy(b_out.at[side, at(0, z.back_stride, z.back)], b_in.at[at(slots[side], z.back_stride, z.back)],
                                    own_sem.at[2 + side]) for side in range(2)]
    s_copy = remote(s_out, s_in, s_send, s_recv, mirror)

    spectrum(x_buf, x_loads, x_out)
    pl.semaphore_wait(barrier, z.owners - 1)
    for side in (1, 0):
        x_kept[side].start()
        each(x_copy(side), 1, z.half_owners, start)
    spectrum(y_buf, y_loads, y_out)

    def place(base, index, pair):
        part, member = index // z.snap_count, index % z.snap_count
        return base(member) + part * z.pair_local + pair

    def gather(source, base, pair, target, block):
        for group in range(z.sets):
            moved = swap_groups([source[pl.ds(place(base, group * z.groups + index, pair), z.tiles, stride=z.kinds), :]
                                 for index in range(z.groups)], z.snap_local)
            for index, piece in enumerate(moved):
                target[pl.ds((block * z.groups + index) * TILE, z.tiles), group * LANES:(group + 1) * LANES] = piece

    batch = min(4, z.half_heights)
    span = batch * z.groups * TILE

    def grams(side):
        found = [None] * z.pair_local
        for block in range(z.half_heights):
            for member in range(z.snap_count):
                step = block * z.snap_count + member
                if step == 0:
                    x_kept[side].wait()
                else:
                    x_copy(side)(step).wait_recv()
            for pair in range(z.pair_local):
                gather(x_in.at[side], lambda member: (block * z.snap_count + member) * z.out_stride, pair, x_rows.at[side, pair], block)
                if block % batch == batch - 1:
                    rows = x_rows[side, pair, pl.ds((block // batch) * span, span), :]
                    term = lax.dot_general(rows, rows, (((0,), (0,)), ((), ())), precision=HIGHEST,
                                           preferred_element_type=jnp.float32)
                    found[pair] = term if found[pair] is None else found[pair] + term
        return [pack([fold(found[index]), fold(found[index + 1])]) for index in range(0, z.pair_local, 2)]

    for index, packed in enumerate(grams(1)):
        g_out[index] = packed
    g_copy.start()
    y_kept.start()
    each(y_copy, 1, z.half_owners, start)
    own_grams = grams(0)
    g_copy.wait_recv()
    tops = [top for index, packed in enumerate(own_grams) for top in unpack(packed + g_in[index])]
    def collect(side):
        which = half if side == 0 else 1 - half
        for pair in range(z.pair_local):
            for block in range(z.half_heights):
                gather(y_in, lambda member: ((block * z.snap_count + member) * 2 + which) * z.out_stride, pair,
                       y_rows.at[side, pair], block)

    small[2].wait()
    ridge = []
    for pair in range(z.pair_local):
        mine = lax.broadcasted_iota(jnp.int32, (1, z.pairs), 1) == pair * z.owners + own_slot
        level = jnp.sum(jnp.where(mine, ridge_ref[...], 0), axis=1, keepdims=True)
        ridge.append(lax.shift_left(jnp.ones_like(level), level).astype(jnp.float32) * (0.25 * z.snaps))
    tops = invert(tops, ridge)
    for index in range(z.pair_local // 2):
        s_out[index] = pack(tops[2 * index:2 * index + 2])
    s_copy.start()

    lane = lax.broadcasted_iota(jnp.int32, (1, LANES), 1)

    def fit(side, tops):
        misses = jnp.zeros((1, 1), jnp.float32)
        energy = jnp.zeros((1, 1), jnp.float32)
        outcome = []
        for pair in range(z.pair_local):
            target = y_rows[side, pair]
            fitted = three(target, embed(tops[pair]))
            gap = target - fitted
            misses = misses + jnp.sum(gap * gap, keepdims=True)
            energy = energy + jnp.sum(target * target, keepdims=True)
            outcome.append(fitted)
        return outcome, jnp.where(lane == 0, misses, jnp.where(lane == 1, energy, 0.0))

    def regroup(side, outcome, note):
        for pair in range(z.pair_local):
            for block in range(z.half_heights):
                for group in range(z.sets):
                    moved = swap_groups([outcome[pair][(block * z.groups + index) * TILE:(block * z.groups + index + 1) * TILE,
                                                       group * LANES:(group + 1) * LANES] for index in range(z.groups)], z.snap_local)
                    for index, piece in enumerate(moved):
                        row = place(lambda member: (block * z.snap_count + member) * z.back_stride, group * z.groups + index, pair)
                        b_out[side, pl.ds(row, z.tiles, stride=z.kinds), :] = piece[:z.tiles]
        b_out[side, pl.ds(z.sent, z.half_owners, stride=z.back_stride), :] = jnp.broadcast_to(note, (z.half_owners, LANES))

    y_kept.wait()
    each(y_copy, 1, z.half_owners, arrived)
    collect(0)
    outcome, note = fit(0, tops)
    regroup(0, outcome, note)
    b_kept[0].start()
    each(b_copy(0, own_slot), 1, z.half_owners, start)
    collect(1)
    s_copy.wait_recv()
    outcome, twin_note = fit(1, [top for index in range(z.pair_local // 2) for top in unpack(s_in[index])])
    note_out[...] = jnp.broadcast_to(note + twin_note, note_out.shape)
    each(note_copy, 0, z.half_owners, start)
    regroup(1, outcome, twin_note)
    b_kept[1].start()
    each(b_copy(1, twin_slot), 1, z.half_owners, start)

    for side in range(2):
        each(x_copy(side), 1, z.half_owners, sent)
    g_copy.wait_send()
    each(y_copy, 1, z.half_owners, sent)
    s_copy.wait_send()
    for side in range(2):
        b_kept[side].wait()
        each(b_copy(side, slots[side]), 1, z.half_owners, arrived)
    each(note_copy, 0, z.half_owners, arrived)

    for tile in range(z.tiles):
        for part in range(2):
            sheet = jnp.concatenate([b_in[pl.ds(tile * z.kinds + part * z.pair_local + pair, z.owners, stride=z.back_stride), :]
                                     for pair in range(z.pair_local)], axis=0)
            turned = sheet.T
            for index in range(z.groups):
                first = (tile * z.groups + index) * 2 + part
                piece = turned[index * z.snap_local:(index + 1) * z.snap_local]
                if z.pairs <= LANES:
                    predicted_ref[pl.ds(first, z.snap_local, stride=2 * z.near), :] = piece
                else:
                    for line in range(z.snap_local):
                        predicted_ref[pl.ds(first + line * 2 * z.near, 1), :] = piece[line:line + 1]
    notes = (jnp.sum(b_in[pl.ds(z.sent, z.owners, stride=z.back_stride), :], axis=0, keepdims=True)
             + jnp.sum(note_in[pl.ds(0, z.half_owners, stride=TILE), :], axis=0, keepdims=True))
    misfit_ref[...] = notes[:, 0:1] / notes[:, 1:2]
    for side in range(2):
        each(b_copy(side, slots[side]), 1, z.half_owners, sent)
    each(note_copy, 0, z.half_owners, sent)


def per_device(resolved, drain, pair_list, ridge_index):
    z = Sizes(resolved.shape, pair_list.shape[0], lax.axis_size("snap"), lax.axis_size("height"))
    vmem = pl.BlockSpec(memory_space=pltpu.VMEM)
    hbm = pl.BlockSpec(memory_space=pltpu.HBM)
    block = (z.snap_local, z.near, z.modes * z.parts, z.points)
    out_rows = z.owners * z.out_stride
    back_rows = z.half_owners * z.back_stride
    gathered = z.groups * TILE
    dma = pltpu.SemaphoreType.DMA
    stay = functools.partial(pltpu.with_memory_space_constraint, memory_space=pltpu.HBM)
    predicted, misfit = pl.pallas_call(
        functools.partial(whole_kernel, z),
        in_specs=[hbm] * 5,
        out_specs=[vmem, vmem],
        out_shape=[jax.ShapeDtypeStruct((z.snap_local * z.near * 2, z.pairs), jnp.float32),
                   jax.ShapeDtypeStruct((1, 1), jnp.float32)],
        scratch_shapes=[
            pltpu.VMEM((2 * z.points, 2 * z.points), jnp.bfloat16),
            pltpu.VMEM((2, z.pairs), jnp.int32),
            pltpu.VMEM((1, z.pairs), jnp.int32),
            pltpu.VMEM(block, jnp.bfloat16),
            pltpu.VMEM(block, jnp.bfloat16),
            pltpu.VMEM((z.columns, z.wide), jnp.bfloat16),
            pltpu.VMEM((out_rows, LANES), jnp.float32),
            pltpu.VMEM((out_rows, LANES), jnp.float32),
            pltpu.VMEM((2, z.half_owners * z.out_stride, LANES), jnp.float32),
            pltpu.VMEM((out_rows, LANES), jnp.float32),
            pltpu.VMEM((2, z.pair_local, z.half_heights * gathered, 2 * z.snaps), jnp.float32),
            pltpu.VMEM((2, z.pair_local, z.half_heights * gathered, 2 * z.snaps), jnp.float32),
            pltpu.VMEM((z.pair_local // 2, z.snaps, 2 * z.snaps), jnp.float32),
            pltpu.VMEM((z.pair_local // 2, z.snaps, 2 * z.snaps), jnp.float32),
            pltpu.VMEM((z.pair_local // 2, z.snaps, 2 * z.snaps), jnp.float32),
            pltpu.VMEM((z.pair_local // 2, z.snaps, 2 * z.snaps), jnp.float32),
            pltpu.VMEM((2, back_rows, LANES), jnp.float32),
            pltpu.VMEM((2 * back_rows, LANES), jnp.float32),
            pltpu.VMEM((TILE, LANES), jnp.float32),
            pltpu.VMEM((z.half_owners * TILE, LANES), jnp.float32),
            dma((2 * z.components + 3,)),
            dma((2, z.half_owners)), dma((2, z.half_owners)),
            dma((z.half_owners,)), dma((z.half_owners,)),
            dma, dma,
            dma, dma,
            dma((2, z.half_owners)), dma((2, z.half_owners)),
            dma((z.half_owners,)), dma((z.half_owners,)),
            dma((5,)),
        ],
        compiler_params=pltpu.CompilerParams(collective_id=0, has_side_effects=True, vmem_limit_bytes=VMEM_BYTES),
    )(stay(jnp.asarray(wave_table(z.points))), stay(pair_list.T), stay(ridge_index.reshape(1, z.pairs)),
      resolved.reshape(block), drain.reshape(block))
    predicted = predicted.reshape(z.snap_local, z.components, z.height_local, 2, z.pairs)
    return (predicted, misfit.reshape(1))


def solution(mesh):
    return jax.shard_map(
        per_device,
        mesh=mesh,
        in_specs=(
            P("snap", None, "height", None, None, None),
            P("snap", None, "height", None, None, None),
            P(),
            P(),
        ),
        out_specs=(P("snap", None, "height", None, None), P()),
        check_vma=False,
    )
```

```python
import functools
import math

import jax
import jax.numpy as jnp
import numpy as np
from jax import lax
from jax.experimental import pallas as pl
from jax.experimental.pallas import tpu as pltpu
from jax.sharding import PartitionSpec as P

HIGHEST = lax.Precision.HIGHEST
LANES = 128
TILE = 8
VMEM_BYTES = 48 << 20
UNROLLED = 16


def wave_table(points):
    grid = np.arange(points)
    theta = (grid[:, None] * grid[None, :] % points).astype(np.float32) * np.float32(2.0 * math.pi / points)
    scaling = np.float32(1.0 / math.sqrt(points))
    cosine = (np.cos(theta) * scaling).T
    sine = (np.sin(theta) * scaling).T
    rows = np.concatenate([np.concatenate([cosine, sine], 1), np.concatenate([-sine, cosine], 1)], 0)
    return rows.astype(jnp.bfloat16)


def round_up(value, unit):
    return -(-value // unit) * unit


def swap_groups(arrays, width):
    arrays = list(arrays)
    lane = lax.broadcasted_iota(jnp.int32, (1, LANES), 1)
    bit = 1
    while bit < len(arrays):
        low = (lane // width) % (2 * bit) < bit
        for index in range(len(arrays)):
            if index & bit:
                continue
            first, second = arrays[index], arrays[index + bit]
            arrays[index] = jnp.where(low, first, pltpu.roll(second, bit * width, 1))
            arrays[index + bit] = jnp.where(low, pltpu.roll(first, LANES - bit * width, 1), second)
        bit *= 2
    return arrays


def fold(whole):
    snaps = whole.shape[0] // 2
    lane = lax.broadcasted_iota(jnp.int32, (snaps, 2 * snaps), 1)
    swapped = pltpu.roll(whole[snaps:], snaps, 1)
    return jnp.where(lane < snaps, whole[:snaps] + swapped, swapped - whole[:snaps])


def invert(grams, ridge):
    pairs = len(grams)
    snaps = grams[0].shape[0]
    lane = lax.broadcasted_iota(jnp.int32, (snaps, 2 * snaps), 1)
    line = lax.broadcasted_iota(jnp.int32, (snaps, 2 * snaps), 0)
    sign = jnp.where(lax.broadcasted_iota(jnp.int32, (1, 2 * snaps), 1) < snaps, -1.0, 1.0)
    states = [grams[pair] + jnp.where(line == lane, ridge[pair], 0.0) for pair in range(pairs)]
    for k in range(0, snaps, 2):
        near, far = line == k, line == k + 1
        column = (lane // 2 == k // 2) | (lane // 2 == (snaps + k) // 2)
        unit = jnp.where((near | far) & (lane == line), 1.0, 0.0)
        for pair in range(pairs):
            state = states[pair]
            first_re, second_re, first_im, second_im = (
                jnp.broadcast_to(state[:, at:at + 1], state.shape) for at in (k, k + 1, snaps + k, snaps + k + 1))
            head, tail = first_re[k:k + 1], second_re[k + 1:k + 2]
            cross_re, cross_im = second_re[k:k + 1], second_im[k:k + 1]
            inverse = 1.0 / (head * tail - (cross_re * cross_re + cross_im * cross_im))
            cleared = jnp.where(column, unit, state)
            one, two = cleared[k:k + 1], cleared[k + 1:k + 2]
            one_twin, two_twin = pltpu.roll(one, snaps, 1) * sign, pltpu.roll(two, snaps, 1) * sign
            top = (tail * one - (cross_re * two + cross_im * two_twin)) * inverse
            top_twin = (tail * one_twin - (cross_re * two_twin - cross_im * two)) * inverse
            low = (head * two - (cross_re * one - cross_im * one_twin)) * inverse
            low_twin = (head * two_twin - (cross_re * one_twin + cross_im * one)) * inverse
            fresh = cleared - ((first_re * top + first_im * top_twin) + (second_re * low + second_im * low_twin))
            states[pair] = jnp.where(near, top, jnp.where(far, low, fresh))
    return [jnp.dot(grams[pair], jnp.concatenate([states[pair], pltpu.roll(states[pair], snaps, 1) * sign], axis=0),
                    precision=HIGHEST, preferred_element_type=jnp.float32) for pair in range(pairs)]


class Sizes:
    def __init__(self, shape, pair_total, snap_count, height_count):
        self.snap_local, self.components, self.height_local, self.modes, self.parts, self.points = shape
        self.snap_count, self.height_count = snap_count, height_count
        self.owners = snap_count * height_count
        self.pairs = pair_total
        self.pair_local = pair_total // self.owners
        self.near = self.components * self.height_local
        self.snaps = snap_count * self.snap_local
        self.groups = LANES // self.snap_local
        self.tiles = self.near // self.groups
        self.tiles_each = self.height_local // self.groups
        self.columns = 2 * self.pairs
        self.kinds = 2 * self.pair_local
        self.sent = self.tiles * self.kinds
        self.out_stride = round_up(self.sent, TILE)
        self.back = self.sent + 1
        self.back_stride = round_up(self.back, TILE)
        self.wide = self.modes * self.parts * self.points
        self.half_heights = height_count // 2
        self.half_owners = snap_count * self.half_heights
        self.sets = 2 * snap_count // self.groups


def three(left, right):
    left_high, right_high = left.astype(jnp.bfloat16), right.astype(jnp.bfloat16)
    left_low = (left - left_high.astype(jnp.float32)).astype(jnp.bfloat16)
    right_low = (right - right_high.astype(jnp.float32)).astype(jnp.bfloat16)
    return lax.dot_general(jnp.concatenate([left_high, left_high, left_low], axis=1),
                           jnp.concatenate([right_high, right_low, right_high], axis=1),
                           (((1,), (1,)), ((), ())), preferred_element_type=jnp.float32)


def embed(top):
    snaps = top.shape[0]
    sign = jnp.where(lax.broadcasted_iota(jnp.int32, (1, 2 * snaps), 1) < snaps, -1.0, 1.0)
    return jnp.concatenate([top, pltpu.roll(top, snaps, 1) * sign], axis=0)


def pack(tops):
    snaps = tops[0].shape[0]
    lane = lax.broadcasted_iota(jnp.int32, (snaps, 2 * snaps), 1)
    line = lax.broadcasted_iota(jnp.int32, (snaps, 2 * snaps), 0)
    first = jnp.where(line >= lane, tops[0], pltpu.roll(tops[0], snaps, 1))
    second = jnp.where(line >= lane - snaps, pltpu.roll(tops[1], snaps, 1), tops[1])
    return jnp.where(lane < snaps, first, second)


def unpack(packed):
    snaps = packed.shape[0]
    lane = lax.broadcasted_iota(jnp.int32, (snaps, snaps), 1)
    line = lax.broadcasted_iota(jnp.int32, (snaps, snaps), 0)
    turned = packed.T
    tops = []
    for pair in range(2):
        plain, other = packed[:, pair * snaps:(pair + 1) * snaps], turned[pair * snaps:(pair + 1) * snaps]
        real = jnp.where(line >= lane, plain, other)
        imaginary = jnp.where(line < lane, plain, jnp.where(line > lane, -other, 0.0))
        tops.append(jnp.concatenate([real, imaginary], axis=1))
    return tops


def whole_kernel(z, wave_hbm, list_hbm, ridge_hbm, x_hbm, y_hbm, predicted_ref, misfit_ref,
                 wave, list_ref, ridge_ref, x_buf, y_buf, table, x_out, y_out, x_in, y_in, x_rows, y_rows, g_out, g_in, s_out, s_in,
                 b_out, b_in, note_out, note_in,
                 load_sem, x_send, x_recv, y_send, y_recv, g_send, g_recv, s_send, s_recv, b_send, b_recv, note_send, note_recv, own_sem):
    snap, height = lax.axis_index("snap"), lax.axis_index("height")
    half, inner = height // z.half_heights, lax.rem(height, z.half_heights)
    own_slot = snap * z.height_count + inner * 2 + half
    twin_slot = snap * z.height_count + inner * 2 + (1 - half)
    barrier = pltpu.get_barrier_semaphore()

    def wrap(value, count):
        return lax.rem(value + count, count)

    def away(step):
        return wrap(snap + lax.rem(step, z.snap_count), z.snap_count), wrap(height + step // z.snap_count, z.height_count)

    def beside(step, sign, side):
        return (wrap(snap + sign * lax.rem(step, z.snap_count), z.snap_count),
                side * z.half_heights + wrap(inner + sign * (step // z.snap_count), z.half_heights))

    def load(source, target, part, index):
        span = pl.ds(part * z.height_local, z.height_local)
        return pltpu.make_async_copy(source.at[:, span], target.at[:, span], load_sem.at[index])

    small = [pltpu.make_async_copy(source, target, load_sem.at[2 * z.components + index])
             for index, (source, target) in enumerate([(list_hbm, list_ref), (wave_hbm, wave), (ridge_hbm, ridge_ref)])]
    for item in small:
        item.start()
    x_loads = [load(x_hbm, x_buf, part, part) for part in range(z.components)]
    y_loads = [load(y_hbm, y_buf, part, z.components + part) for part in range(z.components)]
    for item in x_loads + y_loads:
        item.start()

    def greet(step, carry):
        pl.semaphore_signal(barrier, inc=1, device_id=away(step), device_id_type=pl.DeviceIdType.MESH)
        return carry

    if z.owners > 2 * UNROLLED:
        lax.fori_loop(1, z.owners, greet, 0)
    else:
        for step in range(1, z.owners):
            greet(step, 0)

    same = (lax.broadcasted_iota(jnp.int32, (z.pairs, z.pairs), 0)
            == lax.broadcasted_iota(jnp.int32, (z.pairs, z.pairs), 1))
    small[0].wait()
    mode = jnp.sum(jnp.where(same, list_ref[0:1, :], 0), axis=1, keepdims=True)
    number = jnp.sum(jnp.where(same, list_ref[1:2, :], 0), axis=1, keepdims=True)
    mode = jnp.concatenate([mode, mode], axis=0)
    number = jnp.concatenate([number, number + z.points], axis=0)
    chosen = lax.broadcasted_iota(jnp.int32, (z.columns, 2 * z.points), 1) == number
    small[1].wait()
    picked = jnp.dot(jnp.where(chosen, 1.0, 0.0).astype(jnp.bfloat16), wave[...], preferred_element_type=jnp.float32)
    for index in range(z.modes):
        table[:, index * 2 * z.points:(index + 1) * 2 * z.points] = jnp.where(mode == index, picked, 0.0).astype(jnp.bfloat16)
    x_rows[...] = jnp.zeros_like(x_rows)
    y_rows[...] = jnp.zeros_like(y_rows)

    def spectrum(buf, loads, out):
        for part in range(z.components):
            loads[part].wait()
            rows = jnp.concatenate([buf[:, part * z.height_local + index].reshape(z.snap_local, z.wide)
                                    for index in range(z.height_local)], axis=0)
            product = lax.dot_general(table[...], rows, (((1,), (1,)), ((), ())), preferred_element_type=jnp.float32)
            for each in range(z.tiles_each):
                tile = part * z.tiles_each + each
                for kind in range(z.kinds):
                    out[pl.ds(tile * z.kinds + kind, z.owners, stride=z.out_stride), :] = (
                        product[kind * z.owners:(kind + 1) * z.owners, each * LANES:(each + 1) * LANES])

    def at(index, stride, rows):
        return pl.ds(pl.multiple_of(index * stride, TILE), rows)

    def remote(source, target, send, recv, where):
        return pltpu.make_async_remote_copy(src_ref=source, dst_ref=target, send_sem=send, recv_sem=recv, device_id=where,
                                            device_id_type=pl.DeviceIdType.MESH)

    def each(copy, first, last, act):
        def one(step, carry):
            act(copy(step))
            return carry
        if last > UNROLLED:
            lax.fori_loop(first, last, one, 0)
        else:
            for step in range(first, last):
                act(copy(step))

    def start(item):
        item.start()

    def sent(item):
        item.wait_send()

    def arrived(item):
        item.wait_recv()

    def x_copy(side):
        def copy(step):
            where = beside(step, 1, half)
            slot = where[0] * z.height_count + lax.rem(where[1], z.half_heights) * 2 + (half if side == 0 else 1 - half)
            return remote(x_out.at[at(slot, z.out_stride, z.sent)], x_in.at[side, at(step, z.out_stride, z.sent)],
                          x_send.at[side, step], x_recv.at[side, step], where)
        return copy

    def y_copy(step):
        where = beside(step, 1, half)
        first = where[0] * z.height_count + lax.rem(where[1], z.half_heights) * 2
        return remote(y_out.at[at(first, z.out_stride, 2 * z.out_stride)], y_in.at[at(step, 2 * z.out_stride, 2 * z.out_stride)],
                      y_send.at[step], y_recv.at[step], where)

    def b_copy(side, target):
        def copy(step):
            return remote(b_out.at[side, at(step, z.back_stride, z.back)], b_in.at[at(target, z.back_stride, z.back)],
                          b_send.at[side, step], b_recv.at[side, step], beside(step, -1, half))
        return copy

    def note_copy(step):
        return remote(note_out.at[pl.ds(0, 1)], note_in.at[at(step, TILE, 1)], note_send.at[step], note_recv.at[step],
                      beside(step, 1, 1 - half))

    y_kept = pltpu.make_async_copy(
        y_out.at[at(snap * z.height_count + inner * 2, z.out_stride, 2 * z.out_stride)],
        y_in.at[at(0, 2 * z.out_stride, 2 * z.out_stride)], own_sem.at[1])
    slots = (own_slot, twin_slot)
    x_kept = [pltpu.make_async_copy(x_out.at[at(slots[side], z.out_stride, z.sent)], x_in.at[side, at(0, z.out_stride, z.sent)],
                                    own_sem.at[4 * side]) for side in range(2)]
    mirror = (snap, (1 - half) * z.half_heights + inner)
    g_copy = remote(g_out, g_in, g_send, g_recv, mirror)
    b_kept = [pltpu.make_async_copy(b_out.at[side, at(0, z.back_stride, z.back)], b_in.at[at(slots[side], z.back_stride, z.back)],
                                    own_sem.at[2 + side]) for side in range(2)]
    s_copy = remote(s_out, s_in, s_send, s_recv, mirror)

    spectrum(x_buf, x_loads, x_out)
    pl.semaphore_wait(barrier, z.owners - 1)
    for side in (1, 0):
        x_kept[side].start()
        each(x_copy(side), 1, z.half_owners, start)
    spectrum(y_buf, y_loads, y_out)

    def place(base, index, pair):
        part, member = index // z.snap_count, index % z.snap_count
        return base(member) + part * z.pair_local + pair

    def gather(source, base, pair, target, block):
        for group in range(z.sets):
            moved = swap_groups([source[pl.ds(place(base, group * z.groups + index, pair), z.tiles, stride=z.kinds), :]
                                 for index in range(z.groups)], z.snap_local)
            for index, piece in enumerate(moved):
                target[pl.ds((block * z.groups + index) * TILE, z.tiles), group * LANES:(group + 1) * LANES] = piece

    batch = min(4, z.half_heights)
    span = batch * z.groups * TILE

    def grams(side):
        found = [None] * z.pair_local
        for block in range(z.half_heights):
            for member in range(z.snap_count):
                step = block * z.snap_count + member
                if step == 0:
                    x_kept[side].wait()
                else:
                    x_copy(side)(step).wait_recv()
            for pair in range(z.pair_local):
                gather(x_in.at[side], lambda member: (block * z.snap_count + member) * z.out_stride, pair, x_rows.at[side, pair], block)
                if block % batch == batch - 1:
                    rows = x_rows[side, pair, pl.ds((block // batch) * span, span), :]
                    term = lax.dot_general(rows, rows, (((0,), (0,)), ((), ())), precision=HIGHEST,
                                           preferred_element_type=jnp.float32)
                    found[pair] = term if found[pair] is None else found[pair] + term
        return [pack([fold(found[index]), fold(found[index + 1])]) for index in range(0, z.pair_local, 2)]

    for index, packed in enumerate(grams(1)):
        g_out[index] = packed
    g_copy.start()
    y_kept.start()
    each(y_copy, 1, z.half_owners, start)
    own_grams = grams(0)
    g_copy.wait_recv()
    tops = [top for index, packed in enumerate(own_grams) for top in unpack(packed + g_in[index])]
    def collect(side):
        which = half if side == 0 else 1 - half
        for pair in range(z.pair_local):
            for block in range(z.half_heights):
                gather(y_in, lambda member: ((block * z.snap_count + member) * 2 + which) * z.out_stride, pair,
                       y_rows.at[side, pair], block)

    small[2].wait()
    ridge = []
    for pair in range(z.pair_local):
        mine = lax.broadcasted_iota(jnp.int32, (1, z.pairs), 1) == pair * z.owners + own_slot
        level = jnp.sum(jnp.where(mine, ridge_ref[...], 0), axis=1, keepdims=True)
        ridge.append(lax.shift_left(jnp.ones_like(level), level).astype(jnp.float32) * (0.25 * z.snaps))
    tops = invert(tops, ridge)
    for index in range(z.pair_local // 2):
        s_out[index] = pack(tops[2 * index:2 * index + 2])
    s_copy.start()

    lane = lax.broadcasted_iota(jnp.int32, (1, LANES), 1)

    def fit(side, tops):
        misses = jnp.zeros((1, 1), jnp.float32)
        energy = jnp.zeros((1, 1), jnp.float32)
        outcome = []
        for pair in range(z.pair_local):
            target = y_rows[side, pair]
            fitted = three(target, embed(tops[pair]))
            gap = target - fitted
            misses = misses + jnp.sum(gap * gap, keepdims=True)
            energy = energy + jnp.sum(target * target, keepdims=True)
            outcome.append(fitted)
        return outcome, jnp.where(lane == 0, misses, jnp.where(lane == 1, energy, 0.0))

    def regroup(side, outcome, note):
        for pair in range(z.pair_local):
            for block in range(z.half_heights):
                for group in range(z.sets):
                    moved = swap_groups([outcome[pair][(block * z.groups + index) * TILE:(block * z.groups + index + 1) * TILE,
                                                       group * LANES:(group + 1) * LANES] for index in range(z.groups)], z.snap_local)
                    for index, piece in enumerate(moved):
                        row = place(lambda member: (block * z.snap_count + member) * z.back_stride, group * z.groups + index, pair)
                        b_out[side, pl.ds(row, z.tiles, stride=z.kinds), :] = piece[:z.tiles]
        b_out[side, pl.ds(z.sent, z.half_owners, stride=z.back_stride), :] = jnp.broadcast_to(note, (z.half_owners, LANES))

    y_kept.wait()
    each(y_copy, 1, z.half_owners, arrived)
    collect(0)
    outcome, note = fit(0, tops)
    regroup(0, outcome, note)
    b_kept[0].start()
    each(b_copy(0, own_slot), 1, z.half_owners, start)
    collect(1)
    s_copy.wait_recv()
    outcome, twin_note = fit(1, [top for index in range(z.pair_local // 2) for top in unpack(s_in[index])])
    note_out[...] = jnp.broadcast_to(note + twin_note, note_out.shape)
    each(note_copy, 0, z.half_owners, start)
    regroup(1, outcome, twin_note)
    b_kept[1].start()
    each(b_copy(1, twin_slot), 1, z.half_owners, start)

    for side in range(2):
        each(x_copy(side), 1, z.half_owners, sent)
    g_copy.wait_send()
    each(y_copy, 1, z.half_owners, sent)
    s_copy.wait_send()
    for side in range(2):
        b_kept[side].wait()
        each(b_copy(side, slots[side]), 1, z.half_owners, arrived)
    each(note_copy, 0, z.half_owners, arrived)

    for tile in range(z.tiles):
        for part in range(2):
            sheet = jnp.concatenate([b_in[pl.ds(tile * z.kinds + part * z.pair_local + pair, z.owners, stride=z.back_stride), :]
                                     for pair in range(z.pair_local)], axis=0)
            turned = sheet.T
            for index in range(z.groups):
                first = (tile * z.groups + index) * 2 + part
                piece = turned[index * z.snap_local:(index + 1) * z.snap_local]
                if z.pairs <= LANES:
                    predicted_ref[pl.ds(first, z.snap_local, stride=2 * z.near), :] = piece
                else:
                    for line in range(z.snap_local):
                        predicted_ref[pl.ds(first + line * 2 * z.near, 1), :] = piece[line:line + 1]
    notes = (jnp.sum(b_in[pl.ds(z.sent, z.owners, stride=z.back_stride), :], axis=0, keepdims=True)
             + jnp.sum(note_in[pl.ds(0, z.half_owners, stride=TILE), :], axis=0, keepdims=True))
    misfit_ref[...] = notes[:, 0:1] / notes[:, 1:2]
    for side in range(2):
        each(b_copy(side, slots[side]), 1, z.half_owners, sent)
    each(note_copy, 0, z.half_owners, sent)


def per_device(resolved, drain, pair_list, ridge_index):
    z = Sizes(resolved.shape, pair_list.shape[0], lax.axis_size("snap"), lax.axis_size("height"))
    vmem = pl.BlockSpec(memory_space=pltpu.VMEM)
    hbm = pl.BlockSpec(memory_space=pltpu.HBM)
    block = (z.snap_local, z.near, z.modes * z.parts, z.points)
    out_rows = z.owners * z.out_stride
    back_rows = z.half_owners * z.back_stride
    gathered = z.groups * TILE
    dma = pltpu.SemaphoreType.DMA
    stay = functools.partial(pltpu.with_memory_space_constraint, memory_space=pltpu.HBM)
    predicted, misfit = pl.pallas_call(
        functools.partial(whole_kernel, z),
        in_specs=[hbm] * 5,
        out_specs=[vmem, vmem],
        out_shape=[jax.ShapeDtypeStruct((z.snap_local * z.near * 2, z.pairs), jnp.float32),
                   jax.ShapeDtypeStruct((1, 1), jnp.float32)],
        scratch_shapes=[
            pltpu.VMEM((2 * z.points, 2 * z.points), jnp.bfloat16),
            pltpu.VMEM((2, z.pairs), jnp.int32),
            pltpu.VMEM((1, z.pairs), jnp.int32),
            pltpu.VMEM(block, jnp.bfloat16),
            pltpu.VMEM(block, jnp.bfloat16),
            pltpu.VMEM((z.columns, z.wide), jnp.bfloat16),
            pltpu.VMEM((out_rows, LANES), jnp.float32),
            pltpu.VMEM((out_rows, LANES), jnp.float32),
            pltpu.VMEM((2, z.half_owners * z.out_stride, LANES), jnp.float32),
            pltpu.VMEM((out_rows, LANES), jnp.float32),
            pltpu.VMEM((2, z.pair_local, z.half_heights * gathered, 2 * z.snaps), jnp.float32),
            pltpu.VMEM((2, z.pair_local, z.half_heights * gathered, 2 * z.snaps), jnp.float32),
            pltpu.VMEM((z.pair_local // 2, z.snaps, 2 * z.snaps), jnp.float32),
            pltpu.VMEM((z.pair_local // 2, z.snaps, 2 * z.snaps), jnp.float32),
            pltpu.VMEM((z.pair_local // 2, z.snaps, 2 * z.snaps), jnp.float32),
            pltpu.VMEM((z.pair_local // 2, z.snaps, 2 * z.snaps), jnp.float32),
            pltpu.VMEM((2, back_rows, LANES), jnp.float32),
            pltpu.VMEM((2 * back_rows, LANES), jnp.float32),
            pltpu.VMEM((TILE, LANES), jnp.float32),
            pltpu.VMEM((z.half_owners * TILE, LANES), jnp.float32),
            dma((2 * z.components + 3,)),
            dma((2, z.half_owners)), dma((2, z.half_owners)),
            dma((z.half_owners,)), dma((z.half_owners,)),
            dma, dma,
            dma, dma,
            dma((2, z.half_owners)), dma((2, z.half_owners)),
            dma((z.half_owners,)), dma((z.half_owners,)),
            dma((5,)),
        ],
        compiler_params=pltpu.CompilerParams(collective_id=0, has_side_effects=True, vmem_limit_bytes=VMEM_BYTES),
    )(stay(jnp.asarray(wave_table(z.points))), stay(pair_list.T), stay(ridge_index.reshape(1, z.pairs)),
      resolved.reshape(block), drain.reshape(block))
    predicted = predicted.reshape(z.snap_local, z.components, z.height_local, 2, z.pairs)
    return (predicted, misfit.reshape(1))


def solution(mesh):
    return jax.shard_map(
        per_device,
        mesh=mesh,
        in_specs=(
            P("snap", None, "height", None, None, None),
            P("snap", None, "height", None, None, None),
            P(),
            P(),
        ),
        out_specs=(P("snap", None, "height", None, None), P()),
        check_vma=False,
    )
```
